128 devices in a mesh: lon: 16 (over y, z_hi, core), lat: 8 (over z_lo, x).
Axes of the slice: x: 4, y: 4, z: 4 (z_hi: 2, z_lo: 2; z = z_hi * 2 + z_lo), core: 2. Of those that a mesh axis runs over, the one named last changes fastest.
Arguments:
- members: bfloat16 [3, 256, 2880, 128], P(None, 'lat', 'lon'), may hold values from -6 to 6
- background: bfloat16 [3, 256, 2880], P(None, 'lat', 'lon'), may hold values from -6 to 6
Outputs:
- modes: float32 [3, 256, 2880, 128], P(None, 'lat', 'lon')
- r_factor: float32 [128, 128], replicated
The draws below stay inside these ranges and needn't reach their ends.
All inputs are finite; a program needn't handle non-finite values.
Results may differ from the reference program's by a relative error of at most 0.0076.
The reference program's roundings to bfloat16 on the way (of `anomaly`) count: a program that leaves them out, or rounds other values in their place, can miss the bound.
Values may be sent and summed in bfloat16 or wider, within the bound.
A program may use at most 64 MiB of HBM per device.

```python
import math
import jax
import jax.numpy as jnp
from jax import lax

MEMBERS = 128
FIELDS = 3
LAT = 256
LON = 2880


def shard_levels(key, dims, shards, smallest, top_value):
    loudness = 1.0
    for axis_at, blocks in shards:
        draws = jax.random.uniform(jax.random.fold_in(jax.random.fold_in(key, 6), axis_at), (blocks,), jnp.float32, smallest / len(shards), top_value / len(shards))
        loudness = loudness * jnp.repeat(jnp.exp(draws), dims[axis_at] // blocks).reshape((-1,) + (1,) * (len(dims) - 1 - axis_at))
    return loudness


def centred(stream_key, shape, spread, bound, shards=(), held_as=jnp.bfloat16):
    gain = shard_levels(stream_key, shape, shards, -0.22, 0.18) if shards else 1.0
    entries = jax.random.normal(stream_key, shape, jnp.float32) * spread * gain
    return jnp.minimum(jnp.maximum(entries, -bound), bound).astype(held_as)


def setup_inputs(seed: int = 0) -> dict:
    keys = jax.random.split(jax.random.key(seed), 3)
    members = centred(keys[0], (FIELDS, LAT, LON, MEMBERS), 1.0, 6.0, ((1, 8), (2, 16)))
    background = centred(keys[1], (FIELDS, LAT, LON), 1.0, 6.0, ((1, 8), (2, 16)))
    return {"members": members, "background": background}


def row_coefs(glob, nlat):
    phi = (0.125 * (glob.astype(jnp.float32) + 0.5) - 0.0625 * nlat) * (math.pi / 180.0)
    kx = 0.05 + 0.2 * (1.0 - jnp.cos(phi))
    weight = jnp.sqrt(jnp.cos(phi))
    return (kx.astype(jnp.float32), weight.astype(jnp.float32))

def one_pass(field, kx):
    padded = jnp.pad(field, ((1, 1), (0, 0), (0, 0)))
    padded = jnp.concatenate([padded[:, -1:], padded, padded[:, :1]], axis=1)
    centre = padded[1:-1, 1:-1]
    east_west = padded[1:-1, 2:] + padded[1:-1, :-2] - 2.0 * centre
    north_south = padded[2:, 1:-1] + padded[:-2, 1:-1] - 2.0 * centre
    return centre + kx[:, None, None] * east_west + 0.2 * north_south

def chol_upper(gram):
    order = gram.shape[0]
    index = jnp.arange(order)

    def column(j, lower):
        row_j = lax.dynamic_slice_in_dim(lower, j, 1, 0)[0]
        col_g = lax.dynamic_slice_in_dim(gram, j, 1, 1)[:, 0]
        resid = col_g - jnp.dot(lower, row_j, precision=lax.Precision.HIGHEST)
        pivot = jnp.sqrt(jnp.sum(jnp.where(index == j, resid, 0.0)))
        col_new = jnp.where(index >= j, resid / pivot, 0.0)
        return lower + col_new[:, None] * (index[None, :] == j).astype(jnp.float32)
    lower = lax.fori_loop(0, order, column, jnp.zeros((order, order), jnp.float32))
    return lower.T

def upper_inverse(upper):
    order = upper.shape[0]
    index = jnp.arange(order)
    ident = jnp.eye(order, dtype=jnp.float32)

    def row_step(step, solved):
        i = order - 1 - step
        row_u = lax.dynamic_slice_in_dim(upper, i, 1, 0)[0]
        diag = jnp.sum(jnp.where(index == i, row_u, 0.0))
        above = jnp.where(index > i, row_u, 0.0)
        unit = lax.dynamic_slice_in_dim(ident, i, 1, 0)[0]
        new_row = (unit - jnp.dot(above, solved, precision=lax.Precision.HIGHEST)) / diag
        return solved + (index == i).astype(jnp.float32)[:, None] * new_row[None, :]
    return lax.fori_loop(0, order, row_step, jnp.zeros((order, order), jnp.float32))

def reference(members, background):
    kx, weight = row_coefs(jnp.arange(LAT), LAT)

    def per_field(pair):
        field, ground = pair
        smooth = one_pass(one_pass(field.astype(jnp.float32), kx), kx)
        return ((smooth - ground.astype(jnp.float32)[:, :, None]) * weight[:, None, None]).astype(jnp.bfloat16)
    anomaly = lax.map(per_field, (members, background))
    matrix = anomaly.reshape(-1, MEMBERS)
    gram = jnp.dot(matrix.T, matrix, preferred_element_type=jnp.float32) / (FIELDS * LAT * LON)
    r_factor = chol_upper(gram)
    inverse = upper_inverse(r_factor)
    modes = jnp.dot(matrix, inverse, precision=lax.Precision.HIGHEST, preferred_element_type=jnp.float32)
    return (modes.reshape(FIELDS, LAT, LON, MEMBERS), r_factor)
```

```python
import math

import jax
import jax.numpy as jnp
from jax import lax
from jax.experimental import pallas as pl
from jax.experimental.pallas import tpu as pltpu
from jax.sharding import PartitionSpec as P


def extended(shard, sides, width, wrap):
    for axis, dim in sides:
        peers, length = (lax.axis_size(axis), shard.shape[dim])
        up = [(i, (i + 1) % peers) for i in range(peers if wrap else peers - 1)]
        down = [(j, i) for i, j in up]
        last = lax.slice_in_dim(shard, length - width, length, axis=dim)
        leading = lax.slice_in_dim(shard, 0, width, axis=dim)
        before = lax.ppermute(last, axis, up)
        after = lax.ppermute(leading, axis, down)
        shard = jnp.concatenate([before, shard, after], axis=dim)
    return shard


def row_coefs(glob, nlat):
    phi = (0.125 * (glob.astype(jnp.float32) + 0.5) - 0.0625 * nlat) * (math.pi / 180.0)
    kx = 0.05 + 0.2 * (1.0 - jnp.cos(phi))
    weight = jnp.sqrt(jnp.cos(phi))
    return (kx, weight)


def smooth_pass(padded, kx):
    centre = padded[:, 1:-1, 1:-1]
    east_west = padded[:, 1:-1, 2:] + padded[:, 1:-1, :-2] - 2.0 * centre
    north_south = padded[:, 2:, 1:-1] + padded[:, :-2, 1:-1] - 2.0 * centre
    return centre + kx[None, :, None, None] * east_west + 0.2 * north_south


N = 128
B = 8


def split3(x):
    hi = x.astype(jnp.bfloat16)
    rest = x - hi.astype(jnp.float32)
    mid = rest.astype(jnp.bfloat16)
    lo = (rest - mid.astype(jnp.float32)).astype(jnp.bfloat16)
    return (hi, mid, lo)


def eliminate(w_ref):
    for b0 in range(0, N, B):
        rows = [w_ref[b0 + j : b0 + j + 1, :] for j in range(B)]
        d = {}
        for i in range(B):
            for j in range(i, B):
                d[i, j] = jnp.broadcast_to(rows[i][:, b0 + j : b0 + j + 1], (1, N))
        for j in range(B):
            s = lax.rsqrt(d[j, j])
            u = rows[j] * jnp.concatenate([s, s], axis=1)
            w_ref[b0 + j : b0 + j + 1, :] = u
            l = {i: d[j, i] * s for i in range(j + 1, B)}
            for i in range(j + 1, B):
                for m in range(i, B):
                    d[i, m] = d[i, m] - l[i] * l[m]
                rows[i] = rows[i] - jnp.concatenate([l[i], l[i]], axis=1) * u
        if b0 + B < N:
            hi, mid, lo = split3(w_ref[b0 : b0 + B, :])
            lhs = jnp.concatenate([hi, hi, mid, hi, lo, mid], axis=0)[:, :N]
            rhs = jnp.concatenate([hi, mid, hi, lo, hi, mid], axis=0)
            update = lax.dot_general(
                lhs, rhs, (((0,), (0,)), ((), ())), preferred_element_type=jnp.float32
            )
            w_ref[b0 + B :, :] = w_ref[b0 + B :, :] - update[b0 + B :, :]


def factor_kernel(g_ref, r_ref, x_ref, w_ref):
    row = lax.broadcasted_iota(jnp.int32, (N, N), 0)
    col = lax.broadcasted_iota(jnp.int32, (N, N), 1)
    w_ref[:, :N] = g_ref[...]
    w_ref[:, N:] = (row == col).astype(jnp.float32)
    eliminate(w_ref)
    r_ref[...] = jnp.where(row <= col, w_ref[:, :N], 0.0)
    x_ref[...] = jnp.where(row >= col, w_ref[:, N:], 0.0)


def factor(gram):
    return pl.pallas_call(
        factor_kernel,
        out_shape=[jax.ShapeDtypeStruct((N, N), jnp.float32)] * 2,
        scratch_shapes=[pltpu.VMEM((N, 2 * N), jnp.float32)],
    )(gram)


def local(members, background):
    fields, rows, cols, width = members.shape
    nlat = rows * lax.axis_size("lat")
    first = lax.axis_index("lat") * rows
    kx_rows, unused_weight = row_coefs(first + jnp.arange(rows), nlat)
    padded = extended(members, (("lat", 1),), 1, False)
    padded = extended(padded, (("lon", 2),), 1, True)
    inner = smooth_pass(padded.astype(jnp.float32), kx_rows)
    padded = extended(inner, (("lat", 1),), 1, False)
    padded = extended(padded, (("lon", 2),), 1, True)
    final = smooth_pass(padded, kx_rows)
    unused_kx, weight = row_coefs(first + jnp.arange(rows), nlat)
    anomaly = (
        (final - background.astype(jnp.float32)[:, :, :, None]) * weight[None, :, None, None]
    ).astype(jnp.bfloat16)
    matrix = anomaly.reshape(-1, width)
    partial_gram = lax.dot_general(
        matrix, matrix, (((0,), (0,)), ((), ())), preferred_element_type=jnp.float32
    )
    gram = lax.psum(partial_gram, "lat")
    gram = lax.psum(gram, "lon")
    total_rows = fields * nlat * cols * lax.axis_size("lon")
    gram = gram / total_rows
    r_factor, inverse_t = factor(gram)
    modes = jnp.dot(
        matrix, inverse_t.T, precision=lax.Precision.HIGHEST, preferred_element_type=jnp.float32
    )
    return (modes.reshape(fields, rows, cols, width), r_factor)


def solution(mesh):
    return jax.shard_map(
        local,
        mesh=mesh,
        in_specs=(P(None, "lat", "lon", None), P(None, "lat", "lon")),
        out_specs=(P(None, "lat", "lon", None), P()),
        check_vma=False,
    )
```

```python
import functools
import math

import jax
import jax.numpy as jnp
import numpy as np
from jax import lax
from jax.experimental import pallas as pl
from jax.experimental.pallas import tpu as pltpu
from jax.sharding import PartitionSpec as P

N = 128
B = 8
F, ROWS, COLS = 3, 32, 180
LEFT = 16
PAD = 208
PADS = 216
WIDE = 192
CHUNK = 64
MESH = pl.DeviceIdType.MESH


def split3(x):
    hi = x.astype(jnp.bfloat16)
    rest = x - hi.astype(jnp.float32)
    mid = rest.astype(jnp.bfloat16)
    lo = (rest - mid.astype(jnp.float32)).astype(jnp.bfloat16)
    return (hi, mid, lo)


def eliminate(w_ref):
    for b0 in range(0, N, B):
        rows = [w_ref[b0 + j : b0 + j + 1, :] for j in range(B)]
        d = {}
        for i in range(B):
            for j in range(i, B):
                d[i, j] = jnp.broadcast_to(rows[i][:, b0 + j : b0 + j + 1], (1, N))
        for j in range(B):
            s = lax.rsqrt(d[j, j])
            u = rows[j] * jnp.concatenate([s, s], axis=1)
            w_ref[b0 + j : b0 + j + 1, :] = u
            l = {i: d[j, i] * s for i in range(j + 1, B)}
            for i in range(j + 1, B):
                for m in range(i, B):
                    d[i, m] = d[i, m] - l[i] * l[m]
                rows[i] = rows[i] - jnp.concatenate([l[i], l[i]], axis=1) * u
        if b0 + B < N:
            hi, mid, lo = split3(w_ref[b0 : b0 + B, :])
            lhs = jnp.concatenate([hi, hi, mid, hi, lo, mid], axis=0)[:, :N]
            rhs = jnp.concatenate([hi, mid, hi, lo, hi, mid], axis=0)
            update = lax.dot_general(
                lhs, rhs, (((0,), (0,)), ((), ())), preferred_element_type=jnp.float32
            )
            w_ref[b0 + B :, :] = w_ref[b0 + B :, :] - update[b0 + B :, :]


def row_table(nlat):
    phi = (0.125 * (np.arange(-1, nlat + 1) + 0.5) - 0.0625 * nlat) * (math.pi / 180.0)
    kx = 0.05 + 0.2 * (1.0 - np.cos(phi))
    return np.stack([3.0 - 10.0 * kx, 5.0 * kx, 0.04 * np.sqrt(np.cos(phi))]).astype(np.float32)


def basis_kernel(
    n_lon, n_lat, total,
    m_ref, bg_ref, coef_ref, a_out, r_ref, w_out,
    ub, fu, s1, a_buf, bt, bgp, gram, part, got1, got2, work,
    load_sem, hs_sem, hr_sem, s1_sem, r1_sem, s2_sem, r2_sem, s3_sem, r3_sem, out_sem,
):
    lon, lat = lax.axis_index("lon"), lax.axis_index("lat")
    first = lat * ROWS + 1

    loads = [
        pltpu.make_async_copy(m_ref.at[f], ub.at[f, 2 : 2 + ROWS, LEFT : LEFT + COLS, :], load_sem.at[f])
        for f in range(F)
    ]
    for copy in loads:
        copy.start()

    east, west = lax.rem(lon + 1, n_lon), lax.rem(lon + n_lon - 1, n_lon)
    north, south = lax.rem(lat + n_lat - 1, n_lat), lax.rem(lat + 1, n_lat)

    barrier = pltpu.get_barrier_semaphore()
    for d in range(1, n_lon):
        pl.semaphore_signal(barrier, inc=1, device_id={"lon": lax.rem(lon + d, n_lon), "lat": lat}, device_id_type=MESH)
    for d in range(1, n_lat):
        pl.semaphore_signal(barrier, inc=1, device_id={"lon": lon, "lat": lax.rem(lat + d, n_lat)}, device_id_type=MESH)
    for a in (east, west):
        for b in (north, south):
            pl.semaphore_signal(barrier, inc=1, device_id={"lon": a, "lat": b}, device_id_type=MESH)
    pl.semaphore_wait(barrier, n_lon + n_lat + 2)

    lo_c, hi_c = LEFT - 2, LEFT + COLS
    end_r = 2 + ROWS
    rows = pl.ds(2, ROWS)
    cols = pl.ds(LEFT, COLS)
    plan = [
        (slice(ROWS - 2, ROWS), slice(0, COLS), pl.ds(0, 2), cols, lon, south),
        (slice(0, 2), slice(0, COLS), pl.ds(end_r, 2), cols, lon, north),
        (slice(0, ROWS), slice(COLS - 2, COLS), rows, pl.ds(lo_c, 2), east, lat),
        (slice(0, ROWS), slice(0, 2), rows, pl.ds(hi_c, 2), west, lat),
        (slice(ROWS - 1, ROWS), slice(COLS - 2, COLS), pl.ds(1, 1), pl.ds(lo_c, 2), east, south),
        (slice(ROWS - 1, ROWS), slice(0, 2), pl.ds(1, 1), pl.ds(hi_c, 2), west, south),
        (slice(0, 1), slice(COLS - 2, COLS), pl.ds(end_r, 1), pl.ds(lo_c, 2), east, north),
        (slice(0, 1), slice(0, 2), pl.ds(end_r, 1), pl.ds(hi_c, 2), west, north),
    ]
    halos = [
        pltpu.make_async_remote_copy(
            src_ref=m_ref.at[:, sr, sc, :],
            dst_ref=ub.at[:, dr, dc, :],
            send_sem=hs_sem.at[i],
            recv_sem=hr_sem.at[i],
            device_id={"lon": a, "lat": b},
            device_id_type=MESH,
        )
        for i, (sr, sc, dr, dc, a, b) in enumerate(plan)
    ]
    for i in (2, 3, 0, 1, 4, 5, 6, 7):
        halos[i].start()

    bgp[...] = jnp.zeros_like(bgp)
    for f in range(F):
        bgp[0:ROWS, 0:COLS] = bg_ref[f].astype(jnp.float32) * 25.0
        for h in range(2):
            bt[f, h * N : (h + 1) * N, :] = bgp[:, h * N : (h + 1) * N].T
    gram[...] = jnp.zeros_like(gram)
    keep = lax.broadcasted_iota(jnp.int32, (CHUNK, N), 0) < COLS - 2 * CHUNK

    def widen(f, i):
        fu[f, i] = ub[f, i].astype(jnp.float32)

    def first_pass(f, r, above=None, scale=None):
        ca, ck = coef_ref[0, first + r], coef_ref[1, first + r]
        for c in range(8, 8 + WIDE, CHUNK):
            centre = fu[f, r + 2, c : c + CHUNK]
            sides = fu[f, r + 2, c - 1 : c - 1 + CHUNK] + fu[f, r + 2, c + 1 : c + 1 + CHUNK]
            up, down = fu[f, r + 1, c : c + CHUNK], fu[f, r + 3, c : c + CHUNK]
            if above is not None:
                up, down = above(up, down)
            out = ca * centre + ck * sides + (up + down)
            if scale is not None:
                out = out * scale
            s1[f, r + 1, c : c + CHUNK] = out

    def second_pass(f, r):
        ca, ck, cw = coef_ref[0, first + r], coef_ref[1, first + r], coef_ref[2, first + r]
        for h in range(WIDE // CHUNK):
            c = LEFT + h * CHUNK
            centre = s1[f, r + 1, c : c + CHUNK]
            sides = s1[f, r + 1, c - 1 : c - 1 + CHUNK] + s1[f, r + 1, c + 1 : c + 1 + CHUNK]
            up, down = s1[f, r, c : c + CHUNK], s1[f, r + 2, c : c + CHUNK]
            ground = jnp.broadcast_to(bt[f, h * CHUNK : (h + 1) * CHUNK, r : r + 1], (CHUNK, N))
            out = (ca * centre + ck * sides + (up + down) - ground) * cw
            if h == 2:
                out = jnp.where(keep, out, 0.0)
            a_buf[f, r, h * CHUNK : (h + 1) * CHUNK] = out.astype(jnp.bfloat16)

    def add_gram(f, r, n):
        block = a_buf[f, r : r + n].reshape(n * WIDE, N)
        gram[...] += lax.dot_general(block, block, (((0,), (0,)), ((), ())), preferred_element_type=jnp.float32)

    halos[2].wait()
    halos[3].wait()
    for f in range(F):
        loads[f].wait()

    def interior(f, carry):
        def w(i, c):
            widen(f, i)
            return c

        lax.fori_loop(2, 2 + ROWS, w, 0)

        def p1(r, c):
            first_pass(f, r)
            return c

        lax.fori_loop(1, ROWS - 1, p1, 0)
        for r0 in range(2, ROWS - 2, 7):
            for r in range(r0, r0 + 7):
                second_pass(f, r)
            add_gram(f, r0, 7)
        return carry

    lax.fori_loop(0, F, interior, 0)

    for i in (0, 1, 4, 5, 6, 7):
        halos[i].wait()
    top = jnp.where(lat > 0, 1.0, 0.0).astype(jnp.float32)
    bottom = jnp.where(lat < n_lat - 1, 1.0, 0.0).astype(jnp.float32)

    def border(f, carry):
        for i in (0, 1, ROWS + 2, ROWS + 3):
            widen(f, i)
        first_pass(f, -1, scale=top)
        first_pass(f, 0, above=lambda up, down: (up * top, down))
        first_pass(f, ROWS - 1, above=lambda up, down: (up, down * bottom))
        first_pass(f, ROWS, scale=bottom)
        for r0 in (0, ROWS - 2):
            for r in (r0, r0 + 1):
                second_pass(f, r)
            add_gram(f, r0, 2)
        return carry

    lax.fori_loop(0, F, border, 0)
    store = pltpu.make_async_copy(a_buf, a_out, out_sem)
    store.start()

    size = N // n_lon
    scatter = []
    for d in range(1, n_lon):
        peer = lax.rem(lon + d, n_lon)
        copy = pltpu.make_async_remote_copy(
            src_ref=gram.at[pl.ds(pl.multiple_of(peer * size, size), size), :],
            dst_ref=got1.at[n_lon - 1 - d],
            send_sem=s1_sem.at[d],
            recv_sem=r1_sem.at[d],
            device_id={"lon": peer, "lat": lat},
            device_id_type=MESH,
        )
        copy.start()
        scatter.append(copy)
    mine = pl.ds(pl.multiple_of(lon * size, size), size)
    acc = gram[mine, :]
    for copy in scatter:
        copy.wait()
    for d in range(n_lon - 1):
        acc = acc + got1[d]
    part[...] = acc
    exchange = []
    for d in range(1, n_lat):
        copy = pltpu.make_async_remote_copy(
            src_ref=part,
            dst_ref=got2.at[lat],
            send_sem=s2_sem.at[d],
            recv_sem=r2_sem.at[d],
            device_id={"lon": lon, "lat": lax.rem(lat + d, n_lat)},
            device_id_type=MESH,
        )
        copy.start()
        exchange.append(copy)
    got2[lat] = acc
    for copy in exchange:
        copy.wait()
    acc = got2[0]
    for d in range(1, n_lat):
        acc = acc + got2[d]
    work[mine, 0:N] = acc / total
    gather = []
    for d in range(1, n_lon):
        copy = pltpu.make_async_remote_copy(
            src_ref=work.at[mine, 0:N],
            dst_ref=work.at[mine, 0:N],
            send_sem=s3_sem.at[d],
            recv_sem=r3_sem.at[d],
            device_id={"lon": lax.rem(lon + d, n_lon), "lat": lat},
            device_id_type=MESH,
        )
        copy.start()
        gather.append(copy)
    row = lax.broadcasted_iota(jnp.int32, (N, N), 0)
    col = lax.broadcasted_iota(jnp.int32, (N, N), 1)
    work[:, N:] = (row == col).astype(jnp.float32)
    for copy in gather:
        copy.wait()

    eliminate(work)
    r_ref[...] = jnp.where(row <= col, work[:, :N], 0.0)
    inverse = jnp.where(row >= col, work[:, N:], 0.0).T
    hi, mid, lo = split3(inverse)
    w_out[0:N, 0:N] = hi
    w_out[N:, 0:N] = mid
    w_out[0:N, N:] = lo
    w_out[N:, N:] = jnp.zeros((N, N), jnp.bfloat16)
    store.wait()


def modes_kernel(slabs, a_ref, w_ref, o_ref):
    for s in range(slabs):
        a = a_ref[s]
        out = jnp.dot(jnp.concatenate([a, a], axis=1), w_ref[...], preferred_element_type=jnp.float32)
        o_ref[s] = (out[:, :N] + out[:, N:])[:COLS]


def local(n_lon, n_lat, members, background):
    coefs = jnp.asarray(row_table(n_lat * ROWS))
    size = N // n_lon
    vmem, anywhere = pl.BlockSpec(memory_space=pltpu.VMEM), pl.BlockSpec(memory_space=pl.ANY)
    dma = pltpu.SemaphoreType.DMA
    anomaly, r_factor, weights = pl.pallas_call(
        functools.partial(basis_kernel, n_lon, n_lat, float(F * ROWS * COLS * n_lon * n_lat)),
        out_shape=[
            jax.ShapeDtypeStruct((F, ROWS, WIDE, N), jnp.bfloat16),
            jax.ShapeDtypeStruct((N, N), jnp.float32),
            jax.ShapeDtypeStruct((2 * N, 2 * N), jnp.bfloat16),
        ],
        in_specs=[anywhere, vmem, pl.BlockSpec(memory_space=pltpu.SMEM)],
        out_specs=[anywhere, vmem, vmem],
        scratch_shapes=[
            pltpu.VMEM((F, ROWS + 4, PAD, N), jnp.bfloat16),
            pltpu.VMEM((F, ROWS + 4, PAD, N), jnp.float32),
            pltpu.VMEM((F, ROWS + 2, PADS, N), jnp.float32),
            pltpu.VMEM((F, ROWS, WIDE, N), jnp.bfloat16),
            pltpu.VMEM((F, 2 * N, N), jnp.float32),
            pltpu.VMEM((N, 2 * N), jnp.float32),
            pltpu.VMEM((N, N), jnp.float32),
            pltpu.VMEM((size, N), jnp.float32),
            pltpu.VMEM((n_lon - 1, size, N), jnp.float32),
            pltpu.VMEM((n_lat, size, N), jnp.float32),
            pltpu.VMEM((N, 2 * N), jnp.float32),
            dma((F,)),
            dma((8,)),
            dma((8,)),
            dma((n_lon,)),
            dma((n_lon,)),
            dma((n_lat,)),
            dma((n_lat,)),
            dma((n_lon,)),
            dma((n_lon,)),
            dma(()),
        ],
        compiler_params=pltpu.CompilerParams(
            collective_id=0, has_side_effects=True, vmem_limit_bytes=48 * 1024 * 1024
        ),
        name="basis",
    )(members, background, coefs)
    slabs = 12
    modes = pl.pallas_call(
        functools.partial(modes_kernel, slabs),
        grid=(F * ROWS // slabs,),
        out_shape=jax.ShapeDtypeStruct((F * ROWS, COLS, N), jnp.float32),
        in_specs=[
            pl.BlockSpec((slabs, WIDE, N), lambda i: (i, 0, 0)),
            pl.BlockSpec((2 * N, 2 * N), lambda i: (0, 0)),
        ],
        out_specs=pl.BlockSpec((slabs, COLS, N), lambda i: (i, 0, 0)),
        compiler_params=pltpu.CompilerParams(vmem_limit_bytes=32 * 1024 * 1024),
        name="modes",
    )(anomaly.reshape(F * ROWS, WIDE, N), weights)
    return (modes.reshape(F, ROWS, COLS, N), r_factor)


def solution(mesh):
    return jax.shard_map(
        functools.partial(local, mesh.shape["lon"], mesh.shape["lat"]),
        mesh=mesh,
        in_specs=(P(None, "lat", "lon", None), P(None, "lat", "lon")),
        out_specs=(P(None, "lat", "lon", None), P()),
        check_vma=False,
    )
```

```python
import functools
import math

import jax
import jax.numpy as jnp
import numpy as np
from jax import lax
from jax.experimental import pallas as pl
from jax.experimental.pallas import tpu as pltpu
from jax.sharding import PartitionSpec as P

N = 128
B = 8
F, ROWS, COLS = 3, 32, 180
GROUP = 60
WIN = 40
PACK = 48
MESH = pl.DeviceIdType.MESH


def split3(x):
    hi = x.astype(jnp.bfloat16)
    rest = x - hi.astype(jnp.float32)
    mid = rest.astype(jnp.bfloat16)
    lo = (rest - mid.astype(jnp.float32)).astype(jnp.bfloat16)
    return (hi, mid, lo)


def eliminate(w_ref):
    for b0 in range(0, N, B):
        rows = [w_ref[b0 + j : b0 + j + 1, :] for j in range(B)]
        d = {}
        for i in range(B):
            for j in range(i, B):
                d[i, j] = jnp.broadcast_to(rows[i][:, b0 + j : b0 + j + 1], (1, N))
        for j in range(B):
            s = lax.rsqrt(d[j, j])
            u = rows[j] * jnp.concatenate([s, s], axis=1)
            w_ref[b0 + j : b0 + j + 1, :] = u
            l = {i: d[j, i] * s for i in range(j + 1, B)}
            for i in range(j + 1, B):
                for m in range(i, B):
                    d[i, m] = d[i, m] - l[i] * l[m]
                rows[i] = rows[i] - jnp.concatenate([l[i], l[i]], axis=1) * u
        if b0 + B < N:
            hi, mid, lo = split3(w_ref[b0 : b0 + B, :])
            lhs = jnp.concatenate([hi, hi, mid, hi, lo, mid], axis=0)[:, :N]
            rhs = jnp.concatenate([hi, mid, hi, lo, hi, mid], axis=0)
            update = lax.dot_general(
                lhs, rhs, (((0,), (0,)), ((), ())), preferred_element_type=jnp.float32
            )
            w_ref[b0 + B :, :] = w_ref[b0 + B :, :] - update[b0 + B :, :]


def row_table(nlat):
    glob = np.arange(nlat // ROWS)[:, None] * ROWS + np.arange(-1, WIN - 1)[None, :]

    def of(rows):
        phi = (0.125 * (rows + 0.5) - 0.0625 * nlat) * (math.pi / 180.0)
        return 0.05 + 0.2 * (1.0 - np.cos(phi)), np.sqrt(np.cos(phi))

    kx, _ = of(glob)
    _, weight = of(glob + 1)
    inside = ((glob >= 0) & (glob < nlat)).astype(np.float64)
    table = np.stack([3.0 - 10.0 * kx, 5.0 * kx, inside, 0.04 * weight], axis=1)
    return table.astype(np.float32)


def basis_kernel(
    n_lon, n_lat, total, remote, phases,
    m_ref, bg_ref, coef_ref, a_out, r_ref, w_out,
    ub, fu, s1, a_buf, bt, cf, gram, part, got1, got2, work, bgv,
    load_sem, small_sem, hs_sem, hr_sem, s1_sem, r1_sem, s2_sem, r2_sem, s3_sem, r3_sem, out_sem,
):
    if remote:
        lon, lat = lax.axis_index("lon"), lax.axis_index("lat")
    else:
        lon, lat = 0, 0
    loads = [
        pltpu.make_async_copy(m_ref.at[f], ub.at[f, pl.ds(2, COLS), pl.ds(2, ROWS), :], load_sem.at[f])
        for f in range(F)
    ]
    for copy in loads:
        if "nodma" not in phases:
            copy.start()
    small = [
        pltpu.make_async_copy(bg_ref, bgv, small_sem.at[0]),
        pltpu.make_async_copy(coef_ref.at[lat], cf, small_sem.at[1]),
    ]
    for copy in small:
        copy.start()
    not_first, not_last = lat > 0, lat < n_lat - 1
    halos = []
    if remote:
        east, west = lax.rem(lon + 1, n_lon), lax.rem(lon + n_lon - 1, n_lon)
        north, south = lax.rem(lat + n_lat - 1, n_lat), lax.rem(lat + 1, n_lat)

        barrier = pltpu.get_barrier_semaphore()
        for a in (east, west):
            for b in (north, south):
                pl.semaphore_signal(barrier, inc=1, device_id={"lon": a, "lat": b}, device_id_type=MESH)
        for d in range(1, n_lat):
            pl.semaphore_signal(barrier, inc=1, device_id={"lon": lon, "lat": lax.rem(lat + d, n_lat)}, device_id_type=MESH)
        for d in range(1, n_lon):
            pl.semaphore_signal(barrier, inc=1, device_id={"lon": lax.rem(lon + d, n_lon), "lat": lat}, device_id_type=MESH)
        pl.semaphore_wait(barrier, n_lon + n_lat + 2)

        end = 2 + ROWS
        rows, cols = pl.ds(2, ROWS), pl.ds(2, COLS)
        top, bottom, left, right = pl.ds(0, 2), pl.ds(end, 2), pl.ds(0, 2), pl.ds(2 + COLS, 2)
        left1, right1 = pl.ds(1, 1), pl.ds(2 + COLS, 1)
        plan = [
            (pl.ds(COLS - 2, 2), pl.ds(0, ROWS), left, rows, east, lat, None, None),
            (pl.ds(0, 2), pl.ds(0, ROWS), right, rows, west, lat, None, None),
            (pl.ds(0, COLS), pl.ds(ROWS - 2, 2), cols, top, lon, south, not_last, not_first),
            (pl.ds(0, COLS), pl.ds(0, 2), cols, bottom, lon, north, not_first, not_last),
            (pl.ds(COLS - 1, 1), pl.ds(ROWS - 2, 2), left1, top, east, south, not_last, not_first),
            (pl.ds(0, 1), pl.ds(ROWS - 2, 2), right1, top, west, south, not_last, not_first),
            (pl.ds(COLS - 1, 1), pl.ds(0, 2), left1, bottom, east, north, not_first, not_last),
            (pl.ds(0, 1), pl.ds(0, 2), right1, bottom, west, north, not_first, not_last),
        ]
        for f in range(F):
            for i, (sc, sr, dc, dr, a, b, send, receive) in enumerate(plan):
                copy = pltpu.make_async_remote_copy(
                    src_ref=m_ref.at[f, sc, sr, :],
                    dst_ref=ub.at[f, dc, dr, :],
                    send_sem=hs_sem.at[f, i],
                    recv_sem=hr_sem.at[f, i],
                    device_id={"lon": a, "lat": b},
                    device_id_type=MESH,
                )
                halos.append((f, copy, send, receive))
                if send is None:
                    copy.start()
                else:
                    pl.when(send)(copy.start)

    def finish(f):
        for g, copy, send, receive in halos:
            if g == f:
                if send is None:
                    copy.wait()
                else:
                    pl.when(receive)(copy.wait_recv)
                    pl.when(send)(copy.wait_send)

    def clear(at):
        def body(c, carry):
            for f in range(F):
                ub[f, c, at : at + 2, :] = jnp.zeros((2, N), jnp.bfloat16)
            return carry

        def run():
            lax.fori_loop(0, COLS + 4, body, 0)

        return run

    pl.when(jnp.logical_not(not_first))(clear(0))
    pl.when(jnp.logical_not(not_last))(clear(2 + ROWS))

    for copy in small:
        copy.wait()
    for f in range(F):
        wide = jnp.concatenate([bgv[f].astype(jnp.float32), jnp.zeros((ROWS, 3 * N - COLS), jnp.float32)], axis=1)
        for g in range(COLS // GROUP):
            bt[f, g] = wide[:, g * GROUP : g * GROUP + N]
    gram[...] = jnp.zeros_like(gram)

    def field(f, carry):
        if "convert" in phases:
            def convert(c, carry):
                for k in range(92):
                    fu[c * 92 + k, 0:WIN] = ub[f, c * 92 + k].astype(jnp.float32)[:WIN]
                return carry

            lax.fori_loop(0, (COLS + 4) // 92, convert, 0)

        if "first" in phases:
            def first(g, carry):
                c0 = g * 91
                for t in range(5):
                    at = slice(t * 8 + 1, t * 8 + 9)
                    ca, ck, mask = cf[0, t * 8 : t * 8 + 8], cf[1, t * 8 : t * 8 + 8], cf[2, t * 8 : t * 8 + 8]
                    centre = [fu[c0 + k, at] for k in range(93)]
                    for k in range(91):
                        up, down = fu[c0 + k + 1, t * 8 : t * 8 + 8], fu[c0 + k + 1, t * 8 + 2 : t * 8 + 10]
                        out = ca * centre[k + 1] + ck * (centre[k] + centre[k + 2]) + (up + down)
                        if t in (0, 4):
                            out = out * mask
                        s1[c0 + k, t * 8 : t * 8 + 8] = out
                return carry

            lax.fori_loop(0, (COLS + 2) // 91, first, 0)

        if "second" in phases:
            def second(g, carry):
                c0 = g * GROUP
                lane = lax.broadcasted_iota(jnp.int32, (ROWS, N), 1)
                rows_bg = bt[f, g]
                ones = jnp.ones((N, N), jnp.bfloat16)
                spread = jnp.concatenate([jnp.where(lane == k, rows_bg, 0.0).astype(jnp.bfloat16) for k in range(GROUP)], axis=0)
                grounds = jnp.dot(spread, ones, preferred_element_type=jnp.float32)
                for k in range(GROUP):
                    mid = slice(1, 1 + ROWS)
                    ground = grounds[k * ROWS : (k + 1) * ROWS]
                    out = cf[0, mid] * s1[c0 + k + 1, mid] + cf[1, mid] * (s1[c0 + k, mid] + s1[c0 + k + 2, mid])
                    out = out + (s1[c0 + k + 1, 0:ROWS] + s1[c0 + k + 1, 2 : 2 + ROWS])
                    a_buf[f, c0 + k] = ((out - ground * 25.0) * cf[3, 0:ROWS]).astype(jnp.bfloat16)
                return carry

            lax.fori_loop(0, COLS // GROUP, second, 0)
        if "gram" in phases:
            GC = 180
            def addg(g, carry):
                block = a_buf[f, pl.ds(g * GC, GC)].reshape(GC * ROWS, N)
                gram[...] += lax.dot_general(block, block, (((0,), (0,)), ((), ())), preferred_element_type=jnp.float32)
                return carry
            lax.fori_loop(0, COLS // GC, addg, 0)
        return carry

    stores = []
    for f in range(F):
        if "nodma" not in phases:
            loads[f].wait()
        finish(f)
        field(f, 0)
        store = pltpu.make_async_copy(a_buf.at[f], a_out.at[f], out_sem.at[f])
        if "nodma" not in phases:
            store.start()
            stores.append(store)

    row = lax.broadcasted_iota(jnp.int32, (N, N), 0)
    col = lax.broadcasted_iota(jnp.int32, (N, N), 1)
    work[:, N:] = (row == col).astype(jnp.float32)
    if remote:
        size = N // n_lon
        scatter = []
        for d in range(1, n_lon):
            peer = lax.rem(lon + d, n_lon)
            copy = pltpu.make_async_remote_copy(
                src_ref=gram.at[pl.ds(pl.multiple_of(peer * size, size), size), :],
                dst_ref=got1.at[n_lon - 1 - d],
                send_sem=s1_sem.at[d],
                recv_sem=r1_sem.at[d],
                device_id={"lon": peer, "lat": lat},
                device_id_type=MESH,
            )
            copy.start()
            scatter.append(copy)
        mine = pl.ds(pl.multiple_of(lon * size, size), size)
        acc = gram[mine, :]
        for copy in scatter:
            copy.wait()
        for d in range(n_lon - 1):
            acc = acc + got1[d]
        part[...] = acc
        exchange = []
        for d in range(1, n_lat):
            copy = pltpu.make_async_remote_copy(
                src_ref=part,
                dst_ref=got2.at[lat],
                send_sem=s2_sem.at[d],
                recv_sem=r2_sem.at[d],
                device_id={"lon": lon, "lat": lax.rem(lat + d, n_lat)},
                device_id_type=MESH,
            )
            copy.start()
            exchange.append(copy)
        got2[lat] = acc
        for copy in exchange:
            copy.wait()
        acc = got2[0]
        for d in range(1, n_lat):
            acc = acc + got2[d]
        work[mine, 0:N] = acc / total
        gather = []
        for d in range(1, n_lon):
            copy = pltpu.make_async_remote_copy(
                src_ref=work.at[mine, 0:N],
                dst_ref=work.at[mine, 0:N],
                send_sem=s3_sem.at[d],
                recv_sem=r3_sem.at[d],
                device_id={"lon": lax.rem(lon + d, n_lon), "lat": lat},
                device_id_type=MESH,
            )
            copy.start()
            gather.append(copy)
        for copy in gather:
            copy.wait()
    else:
        work[:, 0:N] = gram[...] / total

    if "chol" in phases:
        eliminate(work)
    r_ref[...] = jnp.where(row <= col, work[:, :N], 0.0)
    inverse = jnp.where(row >= col, work[:, N:], 0.0).T
    hi, mid, lo = split3(inverse)
    w_out[0:N, 0:N] = hi
    w_out[N:, 0:N] = mid
    w_out[0:N, N:] = lo
    w_out[N:, N:] = jnp.zeros((N, N), jnp.bfloat16)
    for store in stores:
        store.wait()


def modes_kernel(a_ref, w_ref, r_in, o_ref, r_out):
    r_out[...] = r_in[...]
    a = a_ref[...]
    out = jnp.dot(jnp.concatenate([a, a], axis=1), w_ref[...], preferred_element_type=jnp.float32)
    o_ref[...] = out[:, :N] + out[:, N:]


ALL = ("convert", "first", "second", "gram", "chol")


def basis(n_lon, n_lat, members, background, remote=True, phases=ALL):
    coefs = jnp.asarray(np.ascontiguousarray(np.broadcast_to(row_table(n_lat * ROWS)[..., None], (n_lat, 4, WIN, N))))
    size = N // n_lon
    vmem, anywhere = pl.BlockSpec(memory_space=pltpu.VMEM), pl.BlockSpec(memory_space=pl.ANY)
    dma = pltpu.SemaphoreType.DMA
    return pl.pallas_call(
        functools.partial(basis_kernel, n_lon, n_lat, float(F * ROWS * COLS * n_lon * n_lat), remote, phases),
        out_shape=[
            jax.ShapeDtypeStruct((F, COLS, ROWS, N), jnp.bfloat16),
            jax.ShapeDtypeStruct((N, N), jnp.float32),
            jax.ShapeDtypeStruct((2 * N, 2 * N), jnp.bfloat16),
        ],
        in_specs=[pl.BlockSpec(memory_space=pltpu.HBM)]*3,
        out_specs=[anywhere, vmem, vmem],
        scratch_shapes=[
            pltpu.VMEM((F, COLS + 4, PACK, N), jnp.bfloat16),
            pltpu.VMEM((COLS + 4, WIN + 8, N), jnp.float32),
            pltpu.VMEM((COLS + 2, WIN, N), jnp.float32),
            pltpu.VMEM((F, COLS, ROWS, N), jnp.bfloat16),
            pltpu.VMEM((F, COLS // GROUP, ROWS, N), jnp.float32),
            pltpu.VMEM((4, WIN, N), jnp.float32),
            pltpu.VMEM((N, N), jnp.float32),
            pltpu.VMEM((size, N), jnp.float32),
            pltpu.VMEM((n_lon, size, N), jnp.float32),
            pltpu.VMEM((n_lat, size, N), jnp.float32),
            pltpu.VMEM((N, 2 * N), jnp.float32),
            pltpu.VMEM((F, ROWS, COLS), jnp.bfloat16),
            dma((F,)),
            dma((2,)),
            dma((F, 8)),
            dma((F, 8)),
            dma((n_lon,)),
            dma((n_lon,)),
            dma((n_lat,)),
            dma((n_lat,)),
            dma((n_lon,)),
            dma((n_lon,)),
            dma((F,)),
        ],
        compiler_params=pltpu.CompilerParams(
            collective_id=0 if remote else None, has_side_effects=True, vmem_limit_bytes=40 * 1024 * 1024
        ),
        name="basis",
    )(pltpu.with_memory_space_constraint(members, pltpu.HBM), pltpu.with_memory_space_constraint(background, pltpu.HBM), pltpu.with_memory_space_constraint(coefs, pltpu.HBM))


def local(n_lon, n_lat, members, background):
    anomaly, r_factor, weights = basis(n_lon, n_lat, jnp.transpose(members, (0, 2, 1, 3)), background)
    total = F * COLS * ROWS
    steps = 12
    modes, r_factor = pl.pallas_call(
        modes_kernel,
        grid=(steps,),
        out_shape=[jax.ShapeDtypeStruct((total, N), jnp.float32), jax.ShapeDtypeStruct((N, N), jnp.float32)],
        in_specs=[
            pl.BlockSpec((total // steps, N), lambda i: (i, 0)),
            pl.BlockSpec((2 * N, 2 * N), lambda i: (0, 0)),
            pl.BlockSpec((N, N), lambda i: (0, 0)),
        ],
        out_specs=[pl.BlockSpec((total // steps, N), lambda i: (i, 0)), pl.BlockSpec((N, N), lambda i: (0, 0))],
        compiler_params=pltpu.CompilerParams(vmem_limit_bytes=16 * 1024 * 1024),
        name="modes",
    )(anomaly.reshape(total, N), weights, r_factor)
    return (jnp.transpose(modes.reshape(F, COLS, ROWS, N), (0, 2, 1, 3)), r_factor)


def solution(mesh):
    return jax.shard_map(
        functools.partial(local, mesh.shape["lon"], mesh.shape["lat"]),
        mesh=mesh,
        in_specs=(P(None, "lat", "lon", None), P(None, "lat", "lon")),
        out_specs=(P(None, "lat", "lon", None), P()),
        check_vma=False,
    )
```

```python
import functools
import math

import jax
import jax.numpy as jnp
import numpy as np
from jax import lax
from jax.experimental import pallas as pl
from jax.experimental.pallas import tpu as pltpu
from jax.sharding import PartitionSpec as P

N = 128
B = 8
F, ROWS, COLS = 3, 32, 180
GROUP = 60
WIN = 40
SIZES = (960,) * 18
MESH = pl.DeviceIdType.MESH


def split3(x):
    hi = x.astype(jnp.bfloat16)
    rest = x - hi.astype(jnp.float32)
    mid = rest.astype(jnp.bfloat16)
    lo = (rest - mid.astype(jnp.float32)).astype(jnp.bfloat16)
    return (hi, mid, lo)


def eliminate(w_ref):
    for b0 in range(0, N, B):
        rows = [w_ref[b0 + j : b0 + j + 1, :] for j in range(B)]
        d = {}
        for i in range(B):
            for j in range(i, B):
                d[i, j] = jnp.broadcast_to(rows[i][:, b0 + j : b0 + j + 1], (1, N))
        for j in range(B):
            s = lax.rsqrt(d[j, j])
            u = rows[j] * jnp.concatenate([s, s], axis=1)
            w_ref[b0 + j : b0 + j + 1, :] = u
            l = {i: d[j, i] * s for i in range(j + 1, B)}
            for i in range(j + 1, B):
                for m in range(i, B):
                    d[i, m] = d[i, m] - l[i] * l[m]
                rows[i] = rows[i] - jnp.concatenate([l[i], l[i]], axis=1) * u
        if b0 + B < N:
            hi, mid, lo = split3(w_ref[b0 : b0 + B, :])
            lhs = jnp.concatenate([hi, hi, mid, hi, lo, mid], axis=0)[:, :N]
            rhs = jnp.concatenate([hi, mid, hi, lo, hi, mid], axis=0)
            update = lax.dot_general(
                lhs, rhs, (((0,), (0,)), ((), ())), preferred_element_type=jnp.float32
            )
            w_ref[b0 + B :, :] = w_ref[b0 + B :, :] - update[b0 + B :, :]


def row_table(nlat):
    glob = np.arange(nlat // ROWS)[:, None] * ROWS + np.arange(-1, WIN - 1)[None, :]

    def of(rows):
        phi = (0.125 * (rows + 0.5) - 0.0625 * nlat) * (math.pi / 180.0)
        return 0.05 + 0.2 * (1.0 - np.cos(phi)), np.sqrt(np.cos(phi))

    kx, _ = of(glob)
    _, weight = of(glob + 1)
    inside = ((glob >= 0) & (glob < nlat)).astype(np.float64)
    table = np.stack([3.0 - 10.0 * kx, 5.0 * kx, inside, 0.04 * weight], axis=1)
    return table.astype(np.float32)


def basis_kernel(
    n_lon, n_lat, total,
    m_ref, bg_ref, coef_ref, a_buf, r_ref, w_out,
    ub, top, bottom, fu, s1, bt, cf, gram, part, got1, got2, work, bgv,
    load_sem, small_sem, hs_sem, hr_sem, s1_sem, r1_sem, s2_sem, r2_sem, s3_sem, r3_sem,
):
    lon, lat = lax.axis_index("lon"), lax.axis_index("lat")
    loads = [
        pltpu.make_async_copy(m_ref.at[f], ub.at[f, pl.ds(2, COLS)], load_sem.at[f])
        for f in range(F)
    ]
    small = [
        pltpu.make_async_copy(bg_ref, bgv, small_sem.at[0]),
        pltpu.make_async_copy(coef_ref.at[lat], cf, small_sem.at[1]),
    ]
    for copy in loads[:1] + small + loads[1:]:
        copy.start()
    not_first, not_last = lat > 0, lat < n_lat - 1
    east, west = lax.rem(lon + 1, n_lon), lax.rem(lon + n_lon - 1, n_lon)
    north, south = lax.rem(lat + n_lat - 1, n_lat), lax.rem(lat + 1, n_lat)

    core, y = lax.rem(lon, 2), lon // 4
    x, z = lax.rem(lat, 4), lax.rem(lon // 2, 2) * 2 + lat // 4

    def in_pair(d):
        core2, x2 = lax.rem(core + d % 2, 2), lax.rem(x + d // 2, 4)
        return core2 + 2 * x2, {"lon": lon - core + core2, "lat": lat - x + x2}

    def in_plane(d):
        y2, z2 = lax.rem(y + d // 4, 4), lax.rem(z + d % 4, 4)
        return {"lon": y2 * 4 + z2 // 2 * 2 + core, "lat": lax.rem(z2, 2) * 4 + x}

    barrier = pltpu.get_barrier_semaphore()
    peers = [{"lon": a, "lat": b} for a in (east, west) for b in (north, south)]
    peers += [{"lon": a, "lat": lat} for a in (east, west)] + [{"lon": lon, "lat": b} for b in (north, south)]
    peers += [in_plane(d) for d in range(1, 16)] + [in_pair(d)[1] for d in range(1, 8)]
    for peer in peers:
        pl.semaphore_signal(barrier, inc=1, device_id=peer, device_id_type=MESH)

    def clear(ref):
        def body(c, carry):
            for f in range(F):
                ref[f, c] = jnp.zeros((2, N), jnp.bfloat16)
            return carry

        def run():
            lax.fori_loop(0, COLS + 4, body, 0)

        return run

    pl.when(jnp.logical_not(not_first))(clear(top))
    pl.when(jnp.logical_not(not_last))(clear(bottom))

    for copy in small:
        copy.wait()
    for f in range(F):
        wide = jnp.concatenate([bgv[f].astype(jnp.float32), jnp.zeros((ROWS, 3 * N - COLS), jnp.float32)], axis=1)
        for g in range(COLS // GROUP):
            bt[f, g] = wide[:, g * GROUP : g * GROUP + N]
    gram[...] = jnp.zeros_like(gram)
    lane = lax.broadcasted_iota(jnp.int32, (16, N), 1)
    ones = jnp.ones((N, N), jnp.bfloat16)

    def first_rows(f, c, t):
        at = pl.ds(8 * t + 7, 8)
        ca, ck = cf[0, 8 * t : 8 * t + 8], cf[1, 8 * t : 8 * t + 8]
        out = ca * fu[f, c + 2, at] + ck * (fu[f, c + 1, at] + fu[f, c + 3, at])
        out = out + (fu[f, c + 2, 8 * t + 6 : 8 * t + 14] + fu[f, c + 2, 8 * t + 8 : 8 * t + 16])
        if t in (0, 4):
            out = out * cf[2, 8 * t : 8 * t + 8]
        s1[f, c + 1, 8 * t : 8 * t + 8] = out

    def second_rows(f, c, t, ground):
        at = slice(8 * t + 1, 8 * t + 9)
        ca, ck, cw = cf[0, at], cf[1, at], cf[3, 8 * t : 8 * t + 8]
        out = ca * s1[f, c + 1, at] + ck * (s1[f, c, at] + s1[f, c + 2, at])
        out = out + (s1[f, c + 1, 8 * t : 8 * t + 8] + s1[f, c + 1, 8 * t + 2 : 8 * t + 10])
        return (out - ground * 25.0) * cw

    def spread(f, g, ks, rows):
        values = jnp.concatenate([bt[f, g, r : r + 8] for r in rows], axis=0)
        picked = [jnp.where(lane == k, values, 0.0).astype(jnp.bfloat16) for k in ks]
        return jnp.dot(jnp.concatenate(picked, axis=0), ones, preferred_element_type=jnp.float32)

    def before(f):
        def widen(i, carry):
            for k in range(90):
                c = i * 90 + k + 2
                fu[f, c, 8 : 8 + ROWS] = ub[f, c].astype(jnp.float32)
            return carry

        lax.fori_loop(0, COLS // 90, widen, 0)

        def first(i, carry):
            for t in (1, 2, 3):
                for k in range(91):
                    first_rows(f, i * 91 + k - 1, t)
            return carry

        lax.fori_loop(0, (COLS + 2) // 91, first, 0)

        def second(g, carry):
            ground = spread(f, g, range(GROUP), (8, 16))
            for k in range(GROUP):
                c = g * GROUP + k
                for t in (1, 2):
                    at = 16 * k + 8 * (t - 1)
                    fu[f, c + 2, 8 * t + 8 : 8 * t + 16] = second_rows(f, c, t, ground[at : at + 8])
            return carry

        lax.fori_loop(0, COLS // GROUP, second, 0)

    def after(f):
        for i in (0, 1, 2, 3, COLS, COLS + 1, COLS + 2, COLS + 3):
            fu[f, i, 8 : 8 + ROWS] = ub[f, i].astype(jnp.float32)
        for c in (-1, 0, COLS - 1, COLS):
            for t in (1, 2, 3):
                first_rows(f, c, t)
        for g, ks in ((0, (0, 1)), (COLS // GROUP - 1, (GROUP - 2, GROUP - 1))):
            ground = spread(f, g, ks, (8, 16))
            for i, k in enumerate(ks):
                c = g * GROUP + k
                for t in (1, 2):
                    at = 16 * i + 8 * (t - 1)
                    fu[f, c + 2, 8 * t + 8 : 8 * t + 16] = second_rows(f, c, t, ground[at : at + 8])

        def widen(i, carry):
            for k in range(91):
                c = i * 91 + k + 1
                fu[f, c, 6:8] = top[f, c].astype(jnp.float32)
                fu[f, c, 8 + ROWS : 10 + ROWS] = bottom[f, c].astype(jnp.float32)
            return carry

        lax.fori_loop(0, (COLS + 2) // 91, widen, 0)

        def first(i, carry):
            for t in (0, 4):
                for k in range(91):
                    first_rows(f, i * 91 + k - 1, t)
            return carry

        lax.fori_loop(0, (COLS + 2) // 91, first, 0)

        def second(g, carry):
            ground = spread(f, g, range(GROUP), (0, 24))
            for k in range(GROUP):
                c = g * GROUP + k
                head = second_rows(f, c, 0, ground[16 * k : 16 * k + 8])
                tail = second_rows(f, c, 3, ground[16 * k + 8 : 16 * k + 16])
                whole = jnp.concatenate([head, fu[f, c + 2, 16:32], tail], axis=0)
                a_buf[f, c] = whole.astype(jnp.bfloat16)
            return carry

        lax.fori_loop(0, COLS // GROUP, second, 0)
        block = a_buf[f].reshape(COLS * ROWS, N)
        gram[...] += lax.dot_general(block, block, (((0,), (0,)), ((), ())), preferred_element_type=jnp.float32)

    loads[0].wait()
    before(0)
    pl.semaphore_wait(barrier, len(peers))

    everyone = (None, None)
    down, up = (not_last, not_first), (not_first, not_last)
    fields, cols = pl.ds(0, F), pl.ds(2, COLS)
    left, right, left1, right1 = pl.ds(0, 2), pl.ds(2 + COLS, 2), pl.ds(1, 1), pl.ds(2 + COLS, 1)
    last2, last1, head2, head1 = pl.ds(COLS - 2, 2), pl.ds(COLS - 1, 1), pl.ds(0, 2), pl.ds(0, 1)
    all_rows, first_two, last_two = pl.ds(0, ROWS), pl.ds(0, 2), pl.ds(ROWS - 2, 2)

    def rows_of(f):
        return [
            (pl.ds(f, 1), pl.ds(0, COLS), last_two, top, cols, lon, south, down),
            (pl.ds(f, 1), pl.ds(0, COLS), first_two, bottom, cols, lon, north, up),
        ]

    plan = rows_of(0) + [
        (fields, last2, all_rows, ub, left, east, lat, everyone),
        (fields, head2, all_rows, ub, right, west, lat, everyone),
        (fields, last1, last_two, top, left1, east, south, down),
        (fields, head1, last_two, top, right1, west, south, down),
        (fields, last1, first_two, bottom, left1, east, north, up),
        (fields, head1, first_two, bottom, right1, west, north, up),
    ] + rows_of(1) + rows_of(2)
    halos = []
    for i, (fs, sc, sr, ref, dc, a, b, (send, receive)) in enumerate(plan):
        copy = pltpu.make_async_remote_copy(
            src_ref=m_ref.at[fs, sc, sr, :],
            dst_ref=ref.at[fs, dc],
            send_sem=hs_sem.at[i],
            recv_sem=hr_sem.at[i],
            device_id={"lon": a, "lat": b},
            device_id_type=MESH,
        )
        halos.append((copy, send, receive))
        if send is None:
            copy.start()
        else:
            pl.when(send)(copy.start)

    def finish(some):
        for copy, send, receive in some:
            if send is None:
                copy.wait()
            else:
                pl.when(receive)(copy.wait_recv)
                pl.when(send)(copy.wait_send)

    for f in (1, 2):
        loads[f].wait()
        before(f)
    for f, some in ((0, halos[:8]), (1, halos[8:10]), (2, halos[10:])):
        finish(some)
        after(f)

    row = lax.broadcasted_iota(jnp.int32, (N, N), 0)
    col = lax.broadcasted_iota(jnp.int32, (N, N), 1)

    size = N // 8

    def rows_at(p):
        return pl.ds(pl.multiple_of(p * size, size), size)

    scatter = []
    for d in range(1, 8):
        place, peer = in_pair(d)
        copy = pltpu.make_async_remote_copy(
            src_ref=gram.at[rows_at(place), :],
            dst_ref=got1.at[d],
            send_sem=s1_sem.at[d],
            recv_sem=r1_sem.at[d],
            device_id=peer,
            device_id_type=MESH,
        )
        copy.start()
        scatter.append(copy)
    mine = rows_at(core + 2 * x)
    work[:, N:] = (row == col).astype(jnp.float32)
    acc = gram[mine, :]
    for copy in scatter:
        copy.wait()
    for d in range(1, 8):
        acc = acc + got1[d]
    part[...] = acc
    slot = y * 4 + z
    exchange = []
    for d in range(1, 16):
        copy = pltpu.make_async_remote_copy(
            src_ref=part,
            dst_ref=got2.at[slot],
            send_sem=s2_sem.at[d],
            recv_sem=r2_sem.at[d],
            device_id=in_plane(d),
            device_id_type=MESH,
        )
        copy.start()
        exchange.append(copy)
    got2[slot] = acc
    for copy in exchange:
        copy.wait()
    sums = [got2[d] for d in range(16)]
    while len(sums) > 1:
        sums = [a + b for a, b in zip(sums[::2], sums[1::2])]
    work[mine, 0:N] = sums[0] / total
    gather = []
    for d in range(1, 8):
        copy = pltpu.make_async_remote_copy(
            src_ref=work.at[mine, 0:N],
            dst_ref=work.at[mine, 0:N],
            send_sem=s3_sem.at[d],
            recv_sem=r3_sem.at[d],
            device_id=in_pair(d)[1],
            device_id_type=MESH,
        )
        copy.start()
        gather.append(copy)
    for copy in gather:
        copy.wait()

    eliminate(work)
    r_ref[...] = jnp.where(row <= col, work[:, :N], 0.0)
    inverse = jnp.where(row >= col, work[:, N:], 0.0).T
    hi, mid, lo = split3(inverse)
    w_out[0:N, 0:N] = hi
    w_out[N:, 0:N] = mid
    w_out[0:N, N:] = lo
    w_out[N:, N:] = jnp.zeros((N, N), jnp.bfloat16)


def modes_kernel(sizes, a_ref, w_ref, r_ref, o_ref, r_out, buf, sem):
    stores, at = [], 0
    for i, size in enumerate(sizes):
        a = a_ref[at : at + size]
        out = jnp.dot(jnp.concatenate([a, a], axis=1), w_ref[...], preferred_element_type=jnp.float32)
        buf[at : at + size] = out[:, :N] + out[:, N:]
        store = pltpu.make_async_copy(buf.at[pl.ds(at, size)], o_ref.at[pl.ds(at, size)], sem.at[i])
        store.start()
        stores.append(store)
        at += size
    r_out[...] = r_ref[...]
    for store in stores:
        store.wait()


def local(n_lon, n_lat, members, background):
    assert n_lon == 16 and n_lat == 8
    coefs = jnp.asarray(np.ascontiguousarray(np.broadcast_to(row_table(n_lat * ROWS)[..., None], (n_lat, 4, WIN, N))))
    vmem, hbm = pl.BlockSpec(memory_space=pltpu.VMEM), pl.BlockSpec(memory_space=pltpu.HBM)
    dma, scratch = pltpu.SemaphoreType.DMA, pltpu.VMEM
    anomaly, r_factor, weights = pl.pallas_call(
        functools.partial(basis_kernel, n_lon, n_lat, float(F * ROWS * COLS * n_lon * n_lat)),
        out_shape=[
            jax.ShapeDtypeStruct((F, COLS, ROWS, N), jnp.bfloat16),
            jax.ShapeDtypeStruct((N, N), jnp.float32),
            jax.ShapeDtypeStruct((2 * N, 2 * N), jnp.bfloat16),
        ],
        in_specs=[hbm, hbm, hbm],
        out_specs=[vmem, vmem, vmem],
        scratch_shapes=[
            scratch((F, COLS + 4, ROWS, N), jnp.bfloat16),
            scratch((F, COLS + 4, 2, N), jnp.bfloat16),
            scratch((F, COLS + 4, 2, N), jnp.bfloat16),
            scratch((F, COLS + 4, WIN + 8, N), jnp.float32),
            scratch((F, COLS + 2, WIN, N), jnp.float32),
            scratch((F, COLS // GROUP, ROWS, N), jnp.float32),
            scratch((4, WIN, N), jnp.float32),
            scratch((N, N), jnp.float32),
            scratch((N // 8, N), jnp.float32),
            scratch((8, N // 8, N), jnp.float32),
            scratch((16, N // 8, N), jnp.float32),
            scratch((N, 2 * N), jnp.float32),
            scratch((F, ROWS, COLS), jnp.bfloat16),
            dma((F,)), dma((2,)), dma((12,)), dma((12,)),
            dma((8,)), dma((8,)), dma((16,)), dma((16,)), dma((8,)), dma((8,)),
        ],
        compiler_params=pltpu.CompilerParams(
            collective_id=0, has_side_effects=True, vmem_limit_bytes=42 * 1024 * 1024
        ),
        name="basis",
    )(*(pltpu.with_memory_space_constraint(a, pltpu.HBM) for a in (jnp.transpose(members, (0, 2, 1, 3)), background, coefs)))
    total = F * COLS * ROWS
    sizes = SIZES
    modes, r_factor = pl.pallas_call(
        functools.partial(modes_kernel, sizes),
        out_shape=[jax.ShapeDtypeStruct((total, N), jnp.float32), jax.ShapeDtypeStruct((N, N), jnp.float32)],
        in_specs=[vmem, vmem, vmem],
        out_specs=[hbm, vmem],
        scratch_shapes=[scratch((total, N), jnp.float32), dma((len(sizes),))],
        compiler_params=pltpu.CompilerParams(vmem_limit_bytes=24 * 1024 * 1024),
        name="modes",
    )(anomaly.reshape(total, N), weights, r_factor)
    return (jnp.transpose(modes.reshape(F, COLS, ROWS, N), (0, 2, 1, 3)), r_factor)


def solution(mesh):
    return jax.shard_map(
        functools.partial(local, mesh.shape["lon"], mesh.shape["lat"]),
        mesh=mesh,
        in_specs=(P(None, "lat", "lon", None), P(None, "lat", "lon")),
        out_specs=(P(None, "lat", "lon", None), P()),
        check_vma=False,
    )
```

```python
import functools
import math

import jax
import jax.numpy as jnp
import numpy as np
from jax import lax
from jax.experimental import pallas as pl
from jax.experimental.pallas import tpu as pltpu
from jax.sharding import PartitionSpec as P

N = 128
B = 16
F, ROWS, COLS = 3, 32, 180
GROUP = 60
WIN = 40
GROUPS = COLS // GROUP
SIZES = (960,) * 18
MESH = pl.DeviceIdType.MESH


def split3(x):
    hi = x.astype(jnp.bfloat16)
    rest = x - hi.astype(jnp.float32)
    mid = rest.astype(jnp.bfloat16)
    lo = (rest - mid.astype(jnp.float32)).astype(jnp.bfloat16)
    return (hi, mid, lo)


def eliminate(w_ref):
    for b0 in range(0, N, B):
        rows = [w_ref[b0 + j : b0 + j + 1, :] for j in range(B)]
        d = {}
        for i in range(B):
            for j in range(i, B):
                d[i, j] = jnp.broadcast_to(rows[i][:, b0 + j : b0 + j + 1], (1, N))
        for j in range(B):
            s = lax.rsqrt(d[j, j])
            u = rows[j] * jnp.concatenate([s, s], axis=1)
            w_ref[b0 + j : b0 + j + 1, :] = u
            l = {i: d[j, i] * s for i in range(j + 1, B)}
            for i in range(j + 1, B):
                for m in range(i, B):
                    d[i, m] = d[i, m] - l[i] * l[m]
                rows[i] = rows[i] - jnp.concatenate([l[i], l[i]], axis=1) * u
        if b0 + B < N:
            hi, mid, lo = split3(w_ref[b0 : b0 + B, :])
            lhs = jnp.concatenate([hi, hi, mid, hi, lo, mid], axis=0)[:, :N]
            rhs = jnp.concatenate([hi, mid, hi, lo, hi, mid], axis=0)
            update = lax.dot_general(
                lhs, rhs, (((0,), (0,)), ((), ())), preferred_element_type=jnp.float32
            )
            w_ref[b0 + B :, :] = w_ref[b0 + B :, :] - update[b0 + B :, :]


def row_table(nlat):
    glob = np.arange(nlat // ROWS)[:, None] * ROWS + np.arange(-1, WIN - 1)[None, :]

    def of(rows):
        phi = (0.125 * (rows + 0.5) - 0.0625 * nlat) * (math.pi / 180.0)
        return 0.05 + 0.2 * (1.0 - np.cos(phi)), np.sqrt(np.cos(phi))

    kx, _ = of(glob)
    _, weight = of(glob + 1)
    inside = ((glob >= 0) & (glob < nlat)).astype(np.float64)
    table = np.stack([3.0 - 10.0 * kx, 5.0 * kx, inside, 0.04 * weight], axis=1)
    return table.astype(np.float32)


def basis_kernel(
    n_lon, n_lat, total,
    m_ref, bg_ref, coef_ref, a_buf, r_ref, w_out,
    ub, edge, fu, s1, bt, hot, cf, gram, part, got1, got2, work, bgv,
    load_sem, small_sem, hs_sem, hr_sem, s1_sem, r1_sem, s2_sem, r2_sem, s3_sem, r3_sem,
):
    lon, lat = lax.axis_index("lon"), lax.axis_index("lat")
    loads = [
        pltpu.make_async_copy(m_ref.at[f], ub.at[f, pl.ds(2, COLS)], load_sem.at[f])
        for f in range(F)
    ]
    small = [
        pltpu.make_async_copy(bg_ref, bgv, small_sem.at[0]),
        pltpu.make_async_copy(coef_ref.at[lat], cf, small_sem.at[1]),
    ]
    for copy in loads[:1] + small + loads[1:]:
        copy.start()
    not_first, not_last = lat > 0, lat < n_lat - 1
    east, west = lax.rem(lon + 1, n_lon), lax.rem(lon + n_lon - 1, n_lon)
    north, south = lax.rem(lat + n_lat - 1, n_lat), lax.rem(lat + 1, n_lat)

    core, y = lax.rem(lon, 2), lon // 4
    x, z = lax.rem(lat, 4), lax.rem(lon // 2, 2) * 2 + lat // 4

    def in_pair(d):
        core2, x2 = lax.rem(core + d % 2, 2), lax.rem(x + d // 2, 4)
        return core2 + 2 * x2, {"lon": lon - core + core2, "lat": lat - x + x2}

    def in_plane(d):
        y2, z2 = lax.rem(y + d // 4, 4), lax.rem(z + d % 4, 4)
        return {"lon": y2 * 4 + z2 // 2 * 2 + core, "lat": lax.rem(z2, 2) * 4 + x}

    barrier = pltpu.get_barrier_semaphore()
    peers = [{"lon": a, "lat": b} for a in (east, west) for b in (north, south)]
    peers += [{"lon": a, "lat": lat} for a in (east, west)] + [{"lon": lon, "lat": b} for b in (north, south)]
    peers += [in_plane(d) for d in range(1, 16)] + [in_pair(d)[1] for d in range(1, 8)]
    for peer in peers:
        pl.semaphore_signal(barrier, inc=1, device_id=peer, device_id_type=MESH)

    def clear(at):
        def body(c, carry):
            for f in range(F):
                edge[f, c, at : at + 2] = jnp.zeros((2, N), jnp.bfloat16)
            return carry

        def run():
            lax.fori_loop(0, COLS + 4, body, 0)

        return run

    pl.when(jnp.logical_not(not_first))(clear(0))
    pl.when(jnp.logical_not(not_last))(clear(2))

    for copy in small:
        copy.wait()
    for f in range(F):
        wide = jnp.concatenate([bgv[f].astype(jnp.float32), jnp.zeros((ROWS, 3 * N - COLS), jnp.float32)], axis=1)
        for g in range(COLS // GROUP):
            part_of = wide[:, g * GROUP : g * GROUP + N]
            bt[f, g, 0] = part_of[8:24].astype(jnp.bfloat16)
            bt[f, g, 1] = jnp.concatenate([part_of[0:8], part_of[24:32]], axis=0).astype(jnp.bfloat16)
    gram[...] = jnp.zeros_like(gram)
    lane = lax.broadcasted_iota(jnp.int32, (16, N), 1)
    for k in range(GROUP):
        hot[k] = jnp.where(lane == k, 1.0, 0.0).astype(jnp.bfloat16)
    scale = jnp.full((N, N), -25.0, jnp.bfloat16)

    def first_rows(f, c0, n, t):
        at = slice(8 * t + 7, 8 * t + 15)
        ca, ck = cf[0, 8 * t : 8 * t + 8], cf[1, 8 * t : 8 * t + 8]
        behind, here = fu[f, c0 + 1, at], fu[f, c0 + 2, at]
        for k in range(n):
            c = c0 + k
            ahead = fu[f, c + 3, at]
            out = ca * here + ck * (behind + ahead)
            out = out + (fu[f, c + 2, 8 * t + 6 : 8 * t + 14] + fu[f, c + 2, 8 * t + 8 : 8 * t + 16])
            if t in (0, 4):
                out = out * cf[2, 8 * t : 8 * t + 8]
            s1[f, c + 1, 8 * t : 8 * t + 8] = out
            behind, here = here, ahead

    def second_rows(f, c0, t):
        at = slice(8 * t + 1, 8 * t + 9)
        ca, ck, cw = cf[0, at], cf[1, at], cf[3, 8 * t : 8 * t + 8]
        held = [s1[f, c0, at], s1[f, c0 + 1, at]]

        def step(k, ground):
            c = c0 + k
            (behind, here), ahead = held, s1[f, c + 2, at]
            out = ca * here + ck * (behind + ahead)
            out = out + (s1[f, c + 1, 8 * t : 8 * t + 8] + s1[f, c + 1, 8 * t + 2 : 8 * t + 10])
            held[:] = [here, ahead]
            return (out + ground) * cw

        return step

    def spread(f, g, ks, half):
        picked = [bt[f, g, half] * hot[k] for k in ks]
        return jnp.dot(jnp.concatenate(picked, axis=0), scale, preferred_element_type=jnp.float32)

    def before(f):
        def widen(i, carry):
            for k in range(90):
                c = i * 90 + k + 2
                fu[f, c, 8 : 8 + ROWS] = ub[f, c].astype(jnp.float32)
            return carry

        lax.fori_loop(0, COLS // 90, widen, 0)

        def first(i, carry):
            for t in (1, 2, 3):
                first_rows(f, i * 91 - 1, 91, t)
            return carry

        lax.fori_loop(0, (COLS + 2) // 91, first, 0)

        def second(g, carry):
            ground = spread(f, g, range(GROUP), 0)
            for t in (1, 2):
                step = second_rows(f, g * GROUP, t)
                for k in range(GROUP):
                    at = 16 * k + 8 * (t - 1)
                    fu[f, g * GROUP + k + 2, 8 * t + 8 : 8 * t + 16] = step(k, ground[at : at + 8])
            return carry

        lax.fori_loop(0, COLS // GROUP, second, 0)

    def after(f):
        for i in (0, 1, 2, 3, COLS, COLS + 1, COLS + 2, COLS + 3):
            fu[f, i, 8 : 8 + ROWS] = ub[f, i].astype(jnp.float32)
        for c in (-1, COLS - 1):
            for t in (1, 2, 3):
                first_rows(f, c, 2, t)
        for g, ks in ((0, (0, 1)), (COLS // GROUP - 1, (GROUP - 2, GROUP - 1))):
            ground = spread(f, g, ks, 0)
            c = g * GROUP + ks[0]
            for t in (1, 2):
                step = second_rows(f, c, t)
                for i in range(len(ks)):
                    at = 16 * i + 8 * (t - 1)
                    fu[f, c + i + 2, 8 * t + 8 : 8 * t + 16] = step(i, ground[at : at + 8])

        def widen(i, carry):
            for k in range(91):
                c = i * 91 + k + 1
                both = edge[f, c].astype(jnp.float32)
                fu[f, c, 6:8] = both[0:2]
                fu[f, c, 8 + ROWS : 10 + ROWS] = both[2:4]
            return carry

        lax.fori_loop(0, (COLS + 2) // 91, widen, 0)

        def first(i, carry):
            for t in (0, 4):
                first_rows(f, i * 91 - 1, 91, t)
            return carry

        lax.fori_loop(0, (COLS + 2) // 91, first, 0)

        def second(g, carry):
            ground = spread(f, g, range(GROUP), 1)
            heads, tails = second_rows(f, g * GROUP, 0), second_rows(f, g * GROUP, 3)
            for k in range(GROUP):
                c = g * GROUP + k
                head = heads(k, ground[16 * k : 16 * k + 8])
                tail = tails(k, ground[16 * k + 8 : 16 * k + 16])
                whole = jnp.concatenate([head, fu[f, c + 2, 16:32], tail], axis=0)
                a_buf[f, c] = whole.astype(jnp.bfloat16)
            return carry

        lax.fori_loop(0, COLS // GROUP, second, 0)

    loads[0].wait()
    before(0)
    pl.semaphore_wait(barrier, len(peers))

    everyone = (None, None)
    down, up = (not_last, not_first), (not_first, not_last)
    fields, cols = pl.ds(0, F), pl.ds(2, COLS)
    left, right, left1, right1 = pl.ds(0, 2), pl.ds(2 + COLS, 2), pl.ds(1, 1), pl.ds(2 + COLS, 1)
    last2, last1, head2, head1 = pl.ds(COLS - 2, 2), pl.ds(COLS - 1, 1), pl.ds(0, 2), pl.ds(0, 1)
    all_rows, first_two, last_two = pl.ds(0, ROWS), pl.ds(0, 2), pl.ds(ROWS - 2, 2)

    def rows_of(f):
        return [
            (pl.ds(f, 1), pl.ds(0, COLS), last_two, 0, cols, lon, south, down),
            (pl.ds(f, 1), pl.ds(0, COLS), first_two, 2, cols, lon, north, up),
        ]

    plan = rows_of(0) + [
        (fields, last2, all_rows, None, left, east, lat, everyone),
        (fields, head2, all_rows, None, right, west, lat, everyone),
        (fields, last1, last_two, 0, left1, east, south, down),
        (fields, head1, last_two, 0, right1, west, south, down),
        (fields, last1, first_two, 2, left1, east, north, up),
        (fields, head1, first_two, 2, right1, west, north, up),
    ] + rows_of(1) + rows_of(2)
    halos = []
    for i, (fs, sc, sr, at, dc, a, b, (send, receive)) in enumerate(plan):
        copy = pltpu.make_async_remote_copy(
            src_ref=m_ref.at[fs, sc, sr, :],
            dst_ref=ub.at[fs, dc] if at is None else edge.at[fs, dc, pl.ds(at, 2), :],
            send_sem=hs_sem.at[i],
            recv_sem=hr_sem.at[i],
            device_id={"lon": a, "lat": b},
            device_id_type=MESH,
        )
        halos.append((copy, send, receive))
        if send is None:
            copy.start()
        else:
            pl.when(send)(copy.start)

    def finish(some):
        for copy, send, receive in some:
            if send is None:
                copy.wait()
            else:
                pl.when(receive)(copy.wait_recv)
                pl.when(send)(copy.wait_send)

    for f in (1, 2):
        loads[f].wait()
        before(f)
    for f, some in ((0, halos[:8]), (1, halos[8:10]), (2, halos[10:])):
        finish(some)
        after(f)
        block = a_buf[f].reshape(COLS * ROWS, N)
        gram[...] += lax.dot_general(block, block, (((0,), (0,)), ((), ())), preferred_element_type=jnp.float32)

    row = lax.broadcasted_iota(jnp.int32, (N, N), 0)
    col = lax.broadcasted_iota(jnp.int32, (N, N), 1)

    size = N // 8

    def rows_at(p):
        return pl.ds(pl.multiple_of(p * size, size), size)

    scatter = []
    for d in range(1, 8):
        place, peer = in_pair(d)
        copy = pltpu.make_async_remote_copy(
            src_ref=gram.at[rows_at(place), :],
            dst_ref=got1.at[d],
            send_sem=s1_sem.at[d],
            recv_sem=r1_sem.at[d],
            device_id=peer,
            device_id_type=MESH,
        )
        copy.start()
        scatter.append(copy)
    mine = rows_at(core + 2 * x)
    work[:, N:] = (row == col).astype(jnp.float32)
    acc = gram[mine, :]
    for copy in scatter:
        copy.wait()
    for d in range(1, 8):
        acc = acc + got1[d]
    part[...] = acc
    slot = y * 4 + z
    exchange = []
    for d in range(1, 16):
        copy = pltpu.make_async_remote_copy(
            src_ref=part,
            dst_ref=got2.at[slot],
            send_sem=s2_sem.at[d],
            recv_sem=r2_sem.at[d],
            device_id=in_plane(d),
            device_id_type=MESH,
        )
        copy.start()
        exchange.append(copy)
    got2[slot] = acc
    for copy in exchange:
        copy.wait()
    sums = [got2[d] for d in range(16)]
    while len(sums) > 1:
        sums = [a + b for a, b in zip(sums[::2], sums[1::2])]
    work[mine, 0:N] = sums[0] / total
    gather = []
    for d in range(1, 8):
        copy = pltpu.make_async_remote_copy(
            src_ref=work.at[mine, 0:N],
            dst_ref=work.at[mine, 0:N],
            send_sem=s3_sem.at[d],
            recv_sem=r3_sem.at[d],
            device_id=in_pair(d)[1],
            device_id_type=MESH,
        )
        copy.start()
        gather.append(copy)
    for copy in gather:
        copy.wait()

    eliminate(work)
    r_ref[...] = jnp.where(row <= col, work[:, :N], 0.0)
    inverse = jnp.where(row >= col, work[:, N:], 0.0).T
    hi, mid, lo = split3(inverse)
    w_out[0:N, 0:N] = hi
    w_out[N:, 0:N] = mid
    w_out[0:N, N:] = lo
    w_out[N:, N:] = jnp.zeros((N, N), jnp.bfloat16)


def modes_kernel(sizes, a_ref, w_ref, r_ref, o_ref, r_out, buf, sem):
    stores, at = [], 0
    for i, size in enumerate(sizes):
        a = a_ref[at : at + size]
        out = jnp.dot(jnp.concatenate([a, a], axis=1), w_ref[...], preferred_element_type=jnp.float32)
        buf[at : at + size] = out[:, :N] + out[:, N:]
        store = pltpu.make_async_copy(buf.at[pl.ds(at, size)], o_ref.at[pl.ds(at, size)], sem.at[i])
        store.start()
        stores.append(store)
        at += size
    r_out[...] = r_ref[...]
    for store in stores:
        store.wait()


def local(n_lon, n_lat, members, background):
    assert n_lon == 16 and n_lat == 8
    coefs = jnp.asarray(np.ascontiguousarray(np.broadcast_to(row_table(n_lat * ROWS)[..., None], (n_lat, 4, WIN, N))))
    vmem, hbm = pl.BlockSpec(memory_space=pltpu.VMEM), pl.BlockSpec(memory_space=pltpu.HBM)
    dma, scratch = pltpu.SemaphoreType.DMA, pltpu.VMEM
    anomaly, r_factor, weights = pl.pallas_call(
        functools.partial(basis_kernel, n_lon, n_lat, float(F * ROWS * COLS * n_lon * n_lat)),
        out_shape=[
            jax.ShapeDtypeStruct((F, COLS, ROWS, N), jnp.bfloat16),
            jax.ShapeDtypeStruct((N, N), jnp.float32),
            jax.ShapeDtypeStruct((2 * N, 2 * N), jnp.bfloat16),
        ],
        in_specs=[hbm, hbm, hbm],
        out_specs=[vmem, vmem, vmem],
        scratch_shapes=[
            scratch((F, COLS + 4, ROWS, N), jnp.bfloat16),
            scratch((F, COLS + 4, 4, N), jnp.bfloat16),
            scratch((F, COLS + 4, WIN + 8, N), jnp.float32),
            scratch((F, COLS + 2, WIN, N), jnp.float32),
            scratch((F, GROUPS, 2, 16, N), jnp.bfloat16),
            scratch((GROUP, 16, N), jnp.bfloat16),
            scratch((4, WIN, N), jnp.float32),
            scratch((N, N), jnp.float32),
            scratch((N // 8, N), jnp.float32),
            scratch((8, N // 8, N), jnp.float32),
            scratch((16, N // 8, N), jnp.float32),
            scratch((N, 2 * N), jnp.float32),
            scratch((F, ROWS, COLS), jnp.bfloat16),
            dma((F,)), dma((2,)), dma((12,)), dma((12,)),
            dma((8,)), dma((8,)), dma((16,)), dma((16,)), dma((8,)), dma((8,)),
        ],
        compiler_params=pltpu.CompilerParams(
            collective_id=0, has_side_effects=True, vmem_limit_bytes=42 * 1024 * 1024
        ),
        name="basis",
    )(*(pltpu.with_memory_space_constraint(a, pltpu.HBM) for a in (jnp.transpose(members, (0, 2, 1, 3)), background, coefs)))
    total = F * COLS * ROWS
    sizes = SIZES
    modes, r_factor = pl.pallas_call(
        functools.partial(modes_kernel, sizes),
        out_shape=[jax.ShapeDtypeStruct((total, N), jnp.float32), jax.ShapeDtypeStruct((N, N), jnp.float32)],
        in_specs=[vmem, vmem, vmem],
        out_specs=[hbm, vmem],
        scratch_shapes=[scratch((total, N), jnp.float32), dma((len(sizes),))],
        compiler_params=pltpu.CompilerParams(vmem_limit_bytes=24 * 1024 * 1024),
        name="modes",
    )(anomaly.reshape(total, N), weights, r_factor)
    return (jnp.transpose(modes.reshape(F, COLS, ROWS, N), (0, 2, 1, 3)), r_factor)


def solution(mesh):
    return jax.shard_map(
        functools.partial(local, mesh.shape["lon"], mesh.shape["lat"]),
        mesh=mesh,
        in_specs=(P(None, "lat", "lon", None), P(None, "lat", "lon")),
        out_specs=(P(None, "lat", "lon", None), P()),
        check_vma=False,
    )
```

```python
import functools
import math

import jax
import jax.numpy as jnp
import numpy as np
from jax import lax
from jax.experimental import pallas as pl
from jax.experimental.pallas import tpu as pltpu
from jax.sharding import PartitionSpec as P

N = 128
B = 16
F, ROWS, COLS = 3, 32, 180
GROUP = 90
WIN = 40
GROUPS = COLS // GROUP
SIZES = (960,) * 18
MESH = pl.DeviceIdType.MESH


def split3(x):
    hi = x.astype(jnp.bfloat16)
    rest = x - hi.astype(jnp.float32)
    mid = rest.astype(jnp.bfloat16)
    lo = (rest - mid.astype(jnp.float32)).astype(jnp.bfloat16)
    return (hi, mid, lo)


def eliminate(w_ref):
    for b0 in range(0, N, B):
        rows = [w_ref[b0 + j : b0 + j + 1, :] for j in range(B)]
        d = {}
        for i in range(B):
            for j in range(i, B):
                d[i, j] = jnp.broadcast_to(rows[i][:, b0 + j : b0 + j + 1], (1, N))
        for j in range(B):
            s = lax.rsqrt(d[j, j])
            u = rows[j] * jnp.concatenate([s, s], axis=1)
            w_ref[b0 + j : b0 + j + 1, :] = u
            l = {i: d[j, i] * s for i in range(j + 1, B)}
            for i in range(j + 1, B):
                for m in range(i, B):
                    d[i, m] = d[i, m] - l[i] * l[m]
                rows[i] = rows[i] - jnp.concatenate([l[i], l[i]], axis=1) * u
        if b0 + B < N:
            hi, mid, lo = split3(w_ref[b0 : b0 + B, :])
            lhs = jnp.concatenate([hi, hi, mid, hi, lo, mid], axis=0)[:, :N]
            rhs = jnp.concatenate([hi, mid, hi, lo, hi, mid], axis=0)
            update = lax.dot_general(
                lhs, rhs, (((0,), (0,)), ((), ())), preferred_element_type=jnp.float32
            )
            w_ref[b0 + B :, :] = w_ref[b0 + B :, :] - update[b0 + B :, :]


def row_table(nlat):
    glob = np.arange(nlat // ROWS)[:, None] * ROWS + np.arange(-1, WIN - 1)[None, :]

    def of(rows):
        phi = (0.125 * (rows + 0.5) - 0.0625 * nlat) * (math.pi / 180.0)
        return 0.05 + 0.2 * (1.0 - np.cos(phi)), np.sqrt(np.cos(phi))

    kx, _ = of(glob)
    _, weight = of(glob + 1)
    inside = ((glob >= 0) & (glob < nlat)).astype(np.float64)
    table = np.stack([3.0 - 10.0 * kx, 5.0 * kx, inside, 0.04 * weight], axis=1)
    return table.astype(np.float32)


def basis_kernel(
    n_lon, n_lat, total,
    m_ref, bg_ref, coef_ref, a_buf, r_ref, w_out,
    ub, edge, fu, s1, bt, hot, cf, gram, part, got1, got2, work, bgv,
    load_sem, small_sem, hs_sem, hr_sem, s1_sem, r1_sem, s2_sem, r2_sem, s3_sem, r3_sem,
):
    lon, lat = lax.axis_index("lon"), lax.axis_index("lat")
    loads = [
        pltpu.make_async_copy(m_ref.at[f], ub.at[f, pl.ds(2, COLS)], load_sem.at[f])
        for f in range(F)
    ]
    small = [
        pltpu.make_async_copy(bg_ref, bgv, small_sem.at[0]),
        pltpu.make_async_copy(coef_ref.at[lat], cf, small_sem.at[1]),
    ]
    for copy in loads[:1] + small + loads[1:]:
        copy.start()
    not_first, not_last = lat > 0, lat < n_lat - 1
    east, west = lax.rem(lon + 1, n_lon), lax.rem(lon + n_lon - 1, n_lon)
    north, south = lax.rem(lat + n_lat - 1, n_lat), lax.rem(lat + 1, n_lat)

    core, y = lax.rem(lon, 2), lon // 4
    x, z = lax.rem(lat, 4), lax.rem(lon // 2, 2) * 2 + lat // 4

    def in_pair(d):
        core2, x2 = lax.rem(core + d % 2, 2), lax.rem(x + d // 2, 4)
        return core2 + 2 * x2, {"lon": lon - core + core2, "lat": lat - x + x2}

    def in_plane(d):
        y2, z2 = lax.rem(y + d // 4, 4), lax.rem(z + d % 4, 4)
        return {"lon": y2 * 4 + z2 // 2 * 2 + core, "lat": lax.rem(z2, 2) * 4 + x}

    barrier = pltpu.get_barrier_semaphore()
    peers = [{"lon": a, "lat": b} for a in (east, west) for b in (north, south)]
    peers += [{"lon": a, "lat": lat} for a in (east, west)] + [{"lon": lon, "lat": b} for b in (north, south)]
    peers += [in_plane(d) for d in range(1, 16)] + [in_pair(d)[1] for d in range(1, 8)]
    for peer in peers:
        pl.semaphore_signal(barrier, inc=1, device_id=peer, device_id_type=MESH)

    def clear(at):
        def body(c, carry):
            for f in range(F):
                edge[f, c, at : at + 2] = jnp.zeros((2, N), jnp.bfloat16)
            return carry

        def run():
            lax.fori_loop(0, COLS + 4, body, 0)

        return run

    pl.when(jnp.logical_not(not_first))(clear(0))
    pl.when(jnp.logical_not(not_last))(clear(2))

    gram[...] = jnp.zeros_like(gram)
    lane = lax.broadcasted_iota(jnp.int32, (16, N), 1)
    for k in range(GROUP):
        hot[k] = jnp.where(lane == k, 1.0, 0.0).astype(jnp.bfloat16)
    scale = jnp.full((N, N), -25.0, jnp.bfloat16)

    for copy in small:
        copy.wait()
    for f in range(F):
        wide = jnp.concatenate([bgv[f].astype(jnp.float32), jnp.zeros((ROWS, 3 * N - COLS), jnp.float32)], axis=1)
        for g in range(COLS // GROUP):
            part_of = wide[:, g * GROUP : g * GROUP + N]
            bt[f, g, 0] = part_of[8:24].astype(jnp.bfloat16)
            bt[f, g, 1] = jnp.concatenate([part_of[0:8], part_of[24:32]], axis=0).astype(jnp.bfloat16)
    def first_rows(f, c0, n, t):
        at = slice(8 * t + 7, 8 * t + 15)
        ca, ck = cf[0, 8 * t : 8 * t + 8], cf[1, 8 * t : 8 * t + 8]
        behind, here = fu[f, c0 + 1, at], fu[f, c0 + 2, at]
        for k in range(n):
            c = c0 + k
            ahead = fu[f, c + 3, at]
            out = ca * here + ck * (behind + ahead)
            out = out + (fu[f, c + 2, 8 * t + 6 : 8 * t + 14] + fu[f, c + 2, 8 * t + 8 : 8 * t + 16])
            if t in (0, 4):
                out = out * cf[2, 8 * t : 8 * t + 8]
            s1[f, c + 1, 8 * t : 8 * t + 8] = out
            behind, here = here, ahead

    def second_rows(f, c0, t):
        at = slice(8 * t + 1, 8 * t + 9)
        ca, ck, cw = cf[0, at], cf[1, at], cf[3, 8 * t : 8 * t + 8]
        held = [s1[f, c0, at], s1[f, c0 + 1, at]]

        def step(k, ground):
            c = c0 + k
            (behind, here), ahead = held, s1[f, c + 2, at]
            out = ca * here + ck * (behind + ahead)
            out = out + (s1[f, c + 1, 8 * t : 8 * t + 8] + s1[f, c + 1, 8 * t + 2 : 8 * t + 10])
            held[:] = [here, ahead]
            return (out + ground) * cw

        return step

    def spread(f, g, ks, half):
        picked = [bt[f, g, half] * hot[k] for k in ks]
        return jnp.dot(jnp.concatenate(picked, axis=0), scale, preferred_element_type=jnp.float32)

    def before(f):
        def widen(i, carry):
            for k in range(90):
                c = i * 90 + k + 2
                fu[f, c, 8 : 8 + ROWS] = ub[f, c].astype(jnp.float32)
            return carry

        lax.fori_loop(0, COLS // 90, widen, 0)

        def first(i, carry):
            for t in (1, 2, 3):
                first_rows(f, i * 91 - 1, 91, t)
            return carry

        lax.fori_loop(0, (COLS + 2) // 91, first, 0)

        def second(g, carry):
            ground = spread(f, g, range(GROUP), 0)
            for t in (1, 2):
                step = second_rows(f, g * GROUP, t)
                for k in range(GROUP):
                    at = 16 * k + 8 * (t - 1)
                    fu[f, g * GROUP + k + 2, 8 * t + 8 : 8 * t + 16] = step(k, ground[at : at + 8])
            return carry

        lax.fori_loop(0, COLS // GROUP, second, 0)

    def after(f):
        for i in (0, 1, 2, 3, COLS, COLS + 1, COLS + 2, COLS + 3):
            fu[f, i, 8 : 8 + ROWS] = ub[f, i].astype(jnp.float32)
        for c in (-1, COLS - 1):
            for t in (1, 2, 3):
                first_rows(f, c, 2, t)
        for g, ks in ((0, (0, 1)), (COLS // GROUP - 1, (GROUP - 2, GROUP - 1))):
            ground = spread(f, g, ks, 0)
            c = g * GROUP + ks[0]
            for t in (1, 2):
                step = second_rows(f, c, t)
                for i in range(len(ks)):
                    at = 16 * i + 8 * (t - 1)
                    fu[f, c + i + 2, 8 * t + 8 : 8 * t + 16] = step(i, ground[at : at + 8])

        def widen(i, carry):
            for k in range(91):
                c = i * 91 + k + 1
                both = edge[f, c].astype(jnp.float32)
                fu[f, c, 6:8] = both[0:2]
                fu[f, c, 8 + ROWS : 10 + ROWS] = both[2:4]
            return carry

        lax.fori_loop(0, (COLS + 2) // 91, widen, 0)

        def first(i, carry):
            for t in (0, 4):
                first_rows(f, i * 91 - 1, 91, t)
            return carry

        lax.fori_loop(0, (COLS + 2) // 91, first, 0)

        def second(g, carry):
            ground = spread(f, g, range(GROUP), 1)
            heads, tails = second_rows(f, g * GROUP, 0), second_rows(f, g * GROUP, 3)
            for k in range(GROUP):
                c = g * GROUP + k
                head = heads(k, ground[16 * k : 16 * k + 8])
                tail = tails(k, ground[16 * k + 8 : 16 * k + 16])
                whole = jnp.concatenate([head, fu[f, c + 2, 16:32], tail], axis=0)
                a_buf[f, c] = whole.astype(jnp.bfloat16)
            return carry

        lax.fori_loop(0, COLS // GROUP, second, 0)

    loads[0].wait()
    before(0)
    pl.semaphore_wait(barrier, len(peers))

    everyone = (None, None)
    down, up = (not_last, not_first), (not_first, not_last)
    fields, cols = pl.ds(0, F), pl.ds(2, COLS)
    left, right, left1, right1 = pl.ds(0, 2), pl.ds(2 + COLS, 2), pl.ds(1, 1), pl.ds(2 + COLS, 1)
    last2, last1, head2, head1 = pl.ds(COLS - 2, 2), pl.ds(COLS - 1, 1), pl.ds(0, 2), pl.ds(0, 1)
    all_rows, first_two, last_two = pl.ds(0, ROWS), pl.ds(0, 2), pl.ds(ROWS - 2, 2)

    def rows_of(f):
        return [
            (pl.ds(f, 1), pl.ds(0, COLS), last_two, 0, cols, lon, south, down),
            (pl.ds(f, 1), pl.ds(0, COLS), first_two, 2, cols, lon, north, up),
        ]

    plan = rows_of(0) + [
        (fields, last2, all_rows, None, left, east, lat, everyone),
        (fields, head2, all_rows, None, right, west, lat, everyone),
        (fields, last1, last_two, 0, left1, east, south, down),
        (fields, head1, last_two, 0, right1, west, south, down),
        (fields, last1, first_two, 2, left1, east, north, up),
        (fields, head1, first_two, 2, right1, west, north, up),
    ] + rows_of(1) + rows_of(2)
    halos = []
    for i, (fs, sc, sr, at, dc, a, b, (send, receive)) in enumerate(plan):
        copy = pltpu.make_async_remote_copy(
            src_ref=m_ref.at[fs, sc, sr, :],
            dst_ref=ub.at[fs, dc] if at is None else edge.at[fs, dc, pl.ds(at, 2), :],
            send_sem=hs_sem.at[i],
            recv_sem=hr_sem.at[i],
            device_id={"lon": a, "lat": b},
            device_id_type=MESH,
        )
        halos.append((copy, send, receive))
        if send is None:
            copy.start()
        else:
            pl.when(send)(copy.start)

    def finish(some):
        for copy, send, receive in some:
            if send is None:
                copy.wait()
            else:
                pl.when(receive)(copy.wait_recv)
                pl.when(send)(copy.wait_send)

    for f in (1, 2):
        loads[f].wait()
        before(f)
    for f, some in ((0, halos[:8]), (1, halos[8:10]), (2, halos[10:])):
        finish(some)
        after(f)
        block = a_buf[f].reshape(COLS * ROWS, N)
        gram[...] += lax.dot_general(block, block, (((0,), (0,)), ((), ())), preferred_element_type=jnp.float32)

    row = lax.broadcasted_iota(jnp.int32, (N, N), 0)
    col = lax.broadcasted_iota(jnp.int32, (N, N), 1)

    size = N // 8

    def rows_at(p):
        return pl.ds(pl.multiple_of(p * size, size), size)

    scatter = []
    for d in range(1, 8):
        place, peer = in_pair(d)
        copy = pltpu.make_async_remote_copy(
            src_ref=gram.at[rows_at(place), :],
            dst_ref=got1.at[d],
            send_sem=s1_sem.at[d],
            recv_sem=r1_sem.at[d],
            device_id=peer,
            device_id_type=MESH,
        )
        copy.start()
        scatter.append(copy)
    mine = rows_at(core + 2 * x)
    work[:, N:] = (row == col).astype(jnp.float32)
    acc = gram[mine, :]
    for copy in scatter:
        copy.wait()
    for d in range(1, 8):
        acc = acc + got1[d]
    part[...] = acc
    slot = y * 4 + z
    exchange = []
    for d in range(1, 16):
        copy = pltpu.make_async_remote_copy(
            src_ref=part,
            dst_ref=got2.at[slot],
            send_sem=s2_sem.at[d],
            recv_sem=r2_sem.at[d],
            device_id=in_plane(d),
            device_id_type=MESH,
        )
        copy.start()
        exchange.append(copy)
    got2[slot] = acc
    for copy in exchange:
        copy.wait()
    sums = [got2[d] for d in range(16)]
    while len(sums) > 1:
        sums = [a + b for a, b in zip(sums[::2], sums[1::2])]
    work[mine, 0:N] = sums[0] / total
    gather = []
    for d in range(1, 8):
        copy = pltpu.make_async_remote_copy(
            src_ref=work.at[mine, 0:N],
            dst_ref=work.at[mine, 0:N],
            send_sem=s3_sem.at[d],
            recv_sem=r3_sem.at[d],
            device_id=in_pair(d)[1],
            device_id_type=MESH,
        )
        copy.start()
        gather.append(copy)
    for copy in gather:
        copy.wait()

    eliminate(work)
    r_ref[...] = jnp.where(row <= col, work[:, :N], 0.0)
    inverse = jnp.where(row >= col, work[:, N:], 0.0).T
    hi, mid, lo = split3(inverse)
    w_out[0:N, 0:N] = hi
    w_out[N:, 0:N] = mid
    w_out[0:N, N:] = lo
    w_out[N:, N:] = jnp.zeros((N, N), jnp.bfloat16)


def modes_kernel(sizes, a_ref, w_ref, r_ref, o_ref, r_out, buf, sem):
    stores, at = [], 0
    for i, size in enumerate(sizes):
        a = a_ref[at : at + size]
        out = jnp.dot(jnp.concatenate([a, a], axis=1), w_ref[...], preferred_element_type=jnp.float32)
        buf[at : at + size] = out[:, :N] + out[:, N:]
        store = pltpu.make_async_copy(buf.at[pl.ds(at, size)], o_ref.at[pl.ds(at, size)], sem.at[i])
        store.start()
        stores.append(store)
        at += size
    r_out[...] = r_ref[...]
    for store in stores:
        store.wait()


def local(n_lon, n_lat, members, background):
    assert n_lon == 16 and n_lat == 8
    coefs = jnp.asarray(np.ascontiguousarray(np.broadcast_to(row_table(n_lat * ROWS)[..., None], (n_lat, 4, WIN, N))))
    vmem, hbm = pl.BlockSpec(memory_space=pltpu.VMEM), pl.BlockSpec(memory_space=pltpu.HBM)
    dma, scratch = pltpu.SemaphoreType.DMA, pltpu.VMEM
    anomaly, r_factor, weights = pl.pallas_call(
        functools.partial(basis_kernel, n_lon, n_lat, float(F * ROWS * COLS * n_lon * n_lat)),
        out_shape=[
            jax.ShapeDtypeStruct((F, COLS, ROWS, N), jnp.bfloat16),
            jax.ShapeDtypeStruct((N, N), jnp.float32),
            jax.ShapeDtypeStruct((2 * N, 2 * N), jnp.bfloat16),
        ],
        in_specs=[hbm, hbm, hbm],
        out_specs=[vmem, vmem, vmem],
        scratch_shapes=[
            scratch((F, COLS + 4, ROWS, N), jnp.bfloat16),
            scratch((F, COLS + 4, 4, N), jnp.bfloat16),
            scratch((F, COLS + 4, WIN + 8, N), jnp.float32),
            scratch((F, COLS + 2, WIN, N), jnp.float32),
            scratch((F, GROUPS, 2, 16, N), jnp.bfloat16),
            scratch((GROUP, 16, N), jnp.bfloat16),
            scratch((4, WIN, N), jnp.float32),
            scratch((N, N), jnp.float32),
            scratch((N // 8, N), jnp.float32),
            scratch((8, N // 8, N), jnp.float32),
            scratch((16, N // 8, N), jnp.float32),
            scratch((N, 2 * N), jnp.float32),
            scratch((F, ROWS, COLS), jnp.bfloat16),
            dma((F,)), dma((2,)), dma((12,)), dma((12,)),
            dma((8,)), dma((8,)), dma((16,)), dma((16,)), dma((8,)), dma((8,)),
        ],
        compiler_params=pltpu.CompilerParams(
            collective_id=0, has_side_effects=True, vmem_limit_bytes=42 * 1024 * 1024
        ),
        name="basis",
    )(*(pltpu.with_memory_space_constraint(a, pltpu.HBM) for a in (jnp.transpose(members, (0, 2, 1, 3)), background, coefs)))
    total = F * COLS * ROWS
    sizes = SIZES
    modes, r_factor = pl.pallas_call(
        functools.partial(modes_kernel, sizes),
        out_shape=[jax.ShapeDtypeStruct((total, N), jnp.float32), jax.ShapeDtypeStruct((N, N), jnp.float32)],
        in_specs=[vmem, vmem, vmem],
        out_specs=[hbm, vmem],
        scratch_shapes=[scratch((total, N), jnp.float32), dma((len(sizes),))],
        compiler_params=pltpu.CompilerParams(vmem_limit_bytes=24 * 1024 * 1024),
        name="modes",
    )(anomaly.reshape(total, N), weights, r_factor)
    return (jnp.transpose(modes.reshape(F, COLS, ROWS, N), (0, 2, 1, 3)), r_factor)


def solution(mesh):
    return jax.shard_map(
        functools.partial(local, mesh.shape["lon"], mesh.shape["lat"]),
        mesh=mesh,
        in_specs=(P(None, "lat", "lon", None), P(None, "lat", "lon")),
        out_specs=(P(None, "lat", "lon", None), P()),
        check_vma=False,
    )
```
